512 devices in a mesh: ctx: 64 (over y, z), head: 8 (over x, core).
Axes of the slice: x: 4, y: 8, z: 8, core: 2. Of those that a mesh axis runs over, the one named last changes fastest.
Arguments:
- queries: bfloat16 [32768, 4096], P('ctx', 'head'), may hold values from -8 to 8
- keys: bfloat16 [32768, 1024], P('ctx', 'head'), may hold values from -6 to 6
- values: bfloat16 [32768, 1024], P('ctx', 'head'), may hold values from -6 to 6
- vertical_blocks: int32 [8, 8], P('head'), may hold values from 0 to 255, as said below
- slash_offsets: int32 [8, 8], P('head'), may hold values from 0 to 16, as said below
- out_weight: bfloat16 [4096, 4096], P(None, 'head'), may hold values from -0.5 to 0.5
Outputs:
- output: bfloat16 [32768, 4096], P('ctx', 'head')
The draws below stay inside these ranges and needn't reach their ends.
Inputs may be any that keep to these rules, and one draw needn't show every extreme that they name: `vertical_blocks`: within each key-value head the 8 entries are distinct; every head lists block 0, and head 0 lists block 255. `slash_offsets`: within each key-value head the 8 offsets are distinct, and every head holds 0 and 16.
All inputs are finite; a program needn't handle non-finite values.
Results may differ from the reference program's by a relative error of at most 0.0057.
Values may be sent and summed in bfloat16 or wider, within the bound.
A program may use at most 64 MiB of HBM per device.

```python
import math
import jax
import jax.numpy as jnp
from jax import lax

D = 4096
NH = 32
KVH = 8
HD = 128
BLK = 128
NV = 8
NS = 8
MAXOFF = 16
TOKENS = 32768
NB = 256


def draw_queries(key, part):
    base_key = jax.random.fold_in(key, 1)
    result = jnp.clip(2.0 * jax.random.normal(base_key, (TOKENS, NH * HD), jnp.float32), -8.0, 8.0)
    return result.astype(jnp.bfloat16)


def draw_keys(key, part):
    base_key = jax.random.fold_in(key, 2)
    result = jnp.clip(jax.random.normal(base_key, (TOKENS, KVH * HD), jnp.float32), -6.0, 6.0)
    return result.astype(jnp.bfloat16)


def draw_vertical_blocks(key, part):

    def one_head(head_id):
        shuffled = jax.random.permutation(jax.random.fold_in(key, 100 + head_id), NB - 2) + 1
        return jnp.concatenate([jnp.zeros((1,), jnp.int32), shuffled[:NV - 1].astype(jnp.int32)])
    table = jax.vmap(one_head)(jnp.arange(KVH))
    return table.at[0, 1].set(NB - 1).astype(jnp.int32)


def draw_slash_offsets(key, part):

    def one_head(head_id):
        shuffled = jax.random.permutation(jax.random.fold_in(key, 200 + head_id), MAXOFF - 1) + 1
        fixed = jnp.array([0, MAXOFF], jnp.int32)
        return jnp.concatenate([fixed, shuffled[:NS - 2].astype(jnp.int32)])
    return jax.vmap(one_head)(jnp.arange(KVH)).astype(jnp.int32)


def levels(key, extent, shards, smallest, largest):
    level, own = 1.0, jax.random.fold_in(key, 6)
    for dim, shards_of in shards:
        draws = jnp.exp(jax.random.uniform(jax.random.fold_in(own, dim), (shards_of,), jnp.float32, smallest / len(shards), largest / len(shards)))
        level = level * jnp.repeat(draws, extent[dim] // shards_of).reshape([-1 if axis == dim else 1 for axis in range(len(extent))])
    return level


def normal_values(key, dims, spread, reach, pieces=(), kind=jnp.bfloat16):
    entries = spread * jax.random.normal(key, dims, jnp.float32)
    if pieces:
        entries = entries * levels(key, dims, pieces, -0.22, 0.18)
    return jnp.clip(entries, -reach, reach).astype(kind)


def setup_inputs(seed: int = 0) -> dict:
    key_list = jax.random.split(jax.random.key(seed), 7)
    return {
        "queries": draw_queries(jax.random.fold_in(key_list[6], 71), 0),
        "keys": draw_keys(jax.random.fold_in(key_list[6], 71), 0),
        "values": normal_values(key_list[2], (TOKENS, KVH * HD), 1.0, 6.0, ((0, 64), (1, 8))),
        "vertical_blocks": draw_vertical_blocks(jax.random.fold_in(key_list[6], 71), 0),
        "slash_offsets": draw_slash_offsets(jax.random.fold_in(key_list[6], 71), 0),
        "out_weight": normal_values(key_list[5], (NH * HD, D), (NH * HD // 32) ** -0.5, 0.5, ((1, 8),)),
    }


def reference(queries, keys, values, vertical_blocks, slash_offsets, out_weight):
    group_size = NH // KVH
    block_count = TOKENS // BLK
    query_blocks = queries.reshape(block_count, BLK, KVH, group_size, HD)
    key_heads = keys.reshape(block_count, BLK, KVH, HD).transpose(2, 0, 1, 3)
    value_heads = values.reshape(block_count, BLK, KVH, HD).transpose(2, 0, 1, 3)
    score_scale = 1.0 / math.sqrt(HD)
    positions = jnp.arange(BLK, dtype=jnp.int32)
    causal = positions[None, :] <= positions[:, None]

    def pick(heads, picks):
        return jnp.take(heads, picks, axis=0)

    def attend(global_block):
        slash_start = global_block - slash_offsets
        repeated = jnp.any(vertical_blocks[:, :, None] == slash_start[:, None, :], 2)
        valid = jnp.concatenate([slash_start >= 0, (vertical_blocks < global_block) & ~repeated], 1)
        diagonal = jnp.concatenate([slash_offsets == 0, jnp.zeros(vertical_blocks.shape, jnp.bool_)], 1)
        chosen = jnp.concatenate([jnp.maximum(slash_start, 0), vertical_blocks], 1).astype(jnp.int32)
        key_sel = jax.vmap(pick)(key_heads, chosen).astype(jnp.float32)
        value_sel = jax.vmap(pick)(value_heads, chosen).astype(jnp.float32)
        rows = query_blocks[global_block].astype(jnp.float32)
        scores = jnp.einsum('rhgd,hjcd->hgrjc', rows, key_sel) * score_scale
        allowed = valid[:, None, None, :, None] & (~diagonal[:, None, None, :, None] | causal[None, None, :, None, :])
        scores = jnp.where(allowed, scores, -1e+30)
        top = lax.optimization_barrier(jnp.max(scores, axis=(3, 4), keepdims=True))
        expo = jnp.exp(scores - top)
        total = lax.optimization_barrier(jnp.sum(expo, axis=(3, 4), keepdims=True))
        weights = (expo / total).astype(jnp.bfloat16)
        return jnp.einsum('hgrjc,hjcd->rhgd', weights.astype(jnp.float32), value_sel).astype(jnp.bfloat16)
    attended = lax.map(attend, jnp.arange(block_count, dtype=jnp.int32)).reshape(TOKENS, NH * HD)
    return jnp.dot(attended, out_weight, preferred_element_type=jnp.float32).astype(jnp.bfloat16)
```

```python
import functools
import math

import jax
import jax.numpy as jnp
from jax import lax
from jax.experimental import pallas as pl
from jax.experimental.pallas import tpu as pltpu
from jax.sharding import Mesh
from jax.sharding import PartitionSpec as P

HD = 128
BLK = 128
LB = 4
GROUP = 4
NV = 8
NS = 8
ROWS = LB * BLK
KEYS = (NV + NS) * BLK
SCALE = math.log2(math.e) / math.sqrt(HD)
MESH = pl.DeviceIdType.MESH
BF16 = jnp.bfloat16
F32 = jnp.float32


def remote(src, dst, send, recv, where):
    return pltpu.make_async_remote_copy(
        src_ref=src, dst_ref=dst, send_sem=send, recv_sem=recv, device_id=where, device_id_type=MESH
    )


def each(lo, hi, do):
    def step(i, carry):
        do(i)
        return carry

    lax.fori_loop(lo, hi, step, 0)


def kernel(
    sizes,
    q_hbm,
    k_hbm,
    v_hbm,
    vb,
    so,
    w_hbm,
    out,
    q,
    w,
    kall,
    vall,
    st1,
    sel,
    st2,
    vert,
    qs,
    ksel,
    vsel,
    s,
    p,
    att,
    s_loc,
    s_a,
    r_a,
    s_b1,
    r_b1,
    s_b2,
    r_b2,
    s_b3,
    r_b3,
    s_b4,
    r_b4,
    s_d,
    r_d,
    r_p,
):
    Y, Z, X = sizes
    y, z, x, c = (lax.axis_index(a) for a in ("y", "z", "x", "core"))
    ctx = y * Z + z
    head = x * 2 + c

    def at_y(i):
        return {"y": i}

    def at_z(i):
        return {"z": i}

    succ = {"y": lax.rem(y + (z + 1) // Z, Y), "z": lax.rem(z + 1, Z)}
    pred = {"y": lax.rem(y + Y - 1 + (z + Z - 1) // Z, Y), "z": lax.rem(z + Z - 1, Z)}
    right, left = {"x": lax.rem(x + 1, X)}, {"x": lax.rem(x + X - 1, X)}
    other = {"core": 1 - c}

    barrier = pltpu.get_barrier_semaphore()

    def greet(where):
        pl.semaphore_signal(barrier, inc=1, device_id=where, device_id_type=MESH)

    each(1, Y, lambda d: greet(at_y(lax.rem(y + d, Y))))
    each(1, Z, lambda d: greet(at_z(lax.rem(z + d, Z))))
    for where in (succ, pred, right, left, other):
        greet(where)
    pl.semaphore_wait(barrier, Y - 1 + Z - 1 + 5)

    def hop(kv, d):
        window = (kall, vall)[kv]
        src = (k_hbm, v_hbm)[kv] if d == 0 else window.at[pl.ds(LB * d, LB)]
        return remote(src, window.at[pl.ds(LB * (d + 1), LB)], s_a.at[kv, d], r_a.at[kv, d], succ)

    def col(kv, to, frm):
        src = (k_hbm, v_hbm)[kv]
        return remote(src.at[:, to], st1.at[kv, frm], s_b1.at[kv, to], r_b1.at[kv, frm], at_y(to))

    def send_col(d):
        to = lax.rem(y + d, Y)
        col(0, to, y).start()
        col(1, to, y).start()

    hop(0, 0).start()
    hop(1, 0).start()
    each(1, Y, send_col)
    local = [
        pltpu.make_async_copy(k_hbm.at[:, y], st1.at[0, y], s_loc.at[0]),
        pltpu.make_async_copy(v_hbm.at[:, y], st1.at[1, y], s_loc.at[1]),
        pltpu.make_async_copy(k_hbm, kall.at[pl.ds(0, LB)], s_loc.at[2]),
        pltpu.make_async_copy(v_hbm, vall.at[pl.ds(0, LB)], s_loc.at[3]),
        pltpu.make_async_copy(q_hbm, q, s_loc.at[4]),
        pltpu.make_async_copy(w_hbm, w, s_loc.at[5]),
    ]
    for copy in local:
        copy.start()

    def wait_col(d):
        frm = lax.rem(y + d, Y)
        col(0, y, frm).wait_recv()
        col(1, y, frm).wait_recv()

    local[0].wait()
    local[1].wait()
    each(1, Y, wait_col)

    for j in range(NV):
        owner = vb[0, j] // LB
        for kv in range(2):
            sel[j, kv] = st1[kv, owner // Z, lax.rem(vb[0, j], LB)]

    def to_row(to, frm):
        return remote(sel.at[to], st2.at[frm], s_b2.at[to], r_b2.at[frm], at_z(to))

    each(1, Z, lambda d: to_row(lax.rem(z + d, Z), z).start())
    st2[z] = sel[z]

    hop(0, 0).wait_recv()
    hop(0, 1).start()
    hop(1, 0).wait_recv()
    hop(1, 1).start()

    each(1, Z, lambda d: to_row(z, lax.rem(z + d, Z)).wait_recv())

    mine = lax.rem(vb[0, z] // LB, Z)
    vert[z, :, y] = st2[mine]

    def along(slot, to):
        here = vert.at[slot, :, y]
        return remote(here, here, s_b3.at[to], r_b3.at[slot], at_z(to))

    def spread(slot, to, frm):
        here = vert.at[slot, :, frm]
        return remote(here, here, s_b4.at[slot, to], r_b4.at[slot, frm], at_y(to))

    def spread_all(slot):
        each(1, Y, lambda d: spread(slot, lax.rem(y + d, Y), y).start())

    each(1, Z, lambda d: along(z, lax.rem(z + d, Z)).start())
    spread_all(z)
    hop(0, 1).wait_recv()
    hop(0, 2).start()
    hop(1, 1).wait_recv()
    hop(1, 2).start()

    def pass_on(d):
        for slot in (lax.rem(z + d, Z), lax.rem(z + Z - d, Z)):
            along(slot, z).wait_recv()
            spread_all(slot)

    each(1, Z // 2, pass_on)
    far = lax.rem(z + Z // 2, Z)
    along(far, z).wait_recv()
    spread_all(far)

    hop(0, 2).wait_recv()
    hop(0, 3).start()
    hop(1, 2).wait_recv()
    hop(1, 3).start()
    for copy in local[2:]:
        copy.wait()

    def wait_slot(slot):
        each(1, Y, lambda d: spread(slot, y, lax.rem(y + d, Y)).wait_recv())

    each(0, NV, wait_slot)
    hop(0, 3).wait_recv()
    hop(1, 3).wait_recv()

    zero_at = 0
    for j in range(NS):
        zero_at += jnp.where(so[0, j] == 0, j, 0)
    ones = jnp.ones((BLK, HD), F32)

    def put(slot, valid, key, value, first):
        rows = pl.ds(slot * BLK, BLK)
        kept = jnp.where(valid, 1.0, 0.0)
        key = key.reshape(BLK, HD).astype(F32)
        value = value.reshape(BLK, HD).astype(F32)
        if first is not None:
            key = key * kept + first * (1.0 - kept)
            value = value * kept
        ksel[rows, :] = key.astype(BF16)
        vsel[rows, pl.ds(0, HD)] = value.astype(BF16)
        vsel[rows, pl.ds(HD, HD)] = (ones * kept).astype(BF16)
        return key

    def attend(i):
        block = ctx * LB + i
        key = put(0, True, kall[i], vall[i], None)
        first = jnp.broadcast_to(key[0:1, :], (BLK, HD))
        for j in range(NS - 1):
            off = so[0, j + jnp.where(zero_at <= j, 1, 0)]
            back = (off - i + LB - 1) // LB
            at = LB * back + (i - off + LB * back)
            put(1 + j, block - off >= 0, kall[at], vall[at], first)
        for j in range(NV):
            seen = vb[0, j]
            valid = seen < block
            for o in range(NS):
                valid = valid & (seen != block - so[0, o])
            put(NS + j, valid, vert[j, 0], vert[j, 1], first)

        for g in range(GROUP):
            qs[pl.ds(g * BLK, BLK), :] = q[pl.ds(i * BLK, BLK), pl.ds(g * HD, HD)]
        top = None
        for j in range(KEYS // 256):
            cols = pl.ds(j * 256, 256)
            part = lax.dot_general(
                qs[...], ksel[cols, :], (((1,), (1,)), ((), ())), preferred_element_type=F32
            )
            if j == 0:
                row = lax.rem(lax.broadcasted_iota(jnp.int32, part.shape, 0), BLK)
                col_at = lax.broadcasted_iota(jnp.int32, part.shape, 1)
                part = jnp.where((col_at <= row) | (col_at >= BLK), part, -1e30)
            s[:, cols] = part
            two = jnp.maximum(part[:, :HD], part[:, HD:])
            top = two if top is None else jnp.maximum(top, two)
        top = jnp.max(top, axis=1, keepdims=True)
        for j in range(KEYS // 256):
            cols = pl.ds(j * 256, 256)
            p[:, cols] = jnp.exp2((s[:, cols] - top) * SCALE).astype(BF16)
        total = jnp.dot(p[...], vsel[...], preferred_element_type=F32)
        total = (total[:, :HD] / total[:, HD:]).astype(BF16)
        for g in range(GROUP):
            att[head, i, :, pl.ds(g * HD, HD)] = total[g * BLK : (g + 1) * BLK, :]

    half = BLK // 2

    def own(n, i):
        here = att.at[head, i]
        where = (right, left, other)[n]
        recv = r_p.at[0, i] if n == 2 else r_d.at[n, i]
        return remote(here, here, s_d.at[n, i], recv, where)

    def chunk(n, i, core):
        frm = lax.rem(x + (X - 1, 1, 2, 2)[n], X) * 2 + core
        rows = (pl.ds(0, BLK), pl.ds(0, BLK), pl.ds(0, half), pl.ds(half, half))[n]
        return att.at[frm, i, rows]

    def got(n, i):
        here = chunk(n, i, c)
        return remote(here, here, s_d.at[0, i], r_d.at[n, i], right)

    def forward(n, i):
        frm = lax.rem(x + (X - 1, 1)[n], X) * 2 + c
        here = att.at[frm, i, pl.ds((0, half)[n], half)]
        return remote(here, here, s_d.at[3 + n, i], r_d.at[2 + n, i], (right, left)[n])

    def share(n, i):
        here = chunk(n, i, c)
        return remote(here, here, s_d.at[5 + n, i], r_p.at[1 + n, i], other)

    def got_other(n, i):
        here = att.at[x * 2 + 1 - c, i] if n == 0 else chunk(n - 1, i, 1 - c)
        return remote(here, here, s_d.at[0, i], r_p.at[n, i], other)

    def relay_near(i):
        for n in range(2):
            got(n, i).wait_recv()
            forward(n, i).start()
            share(n, i).start()

    def relay_far(i):
        for n in range(2, 4):
            got(n, i).wait_recv()
            share(n, i).start()

    def project(i):
        for n in range(5):
            got_other(n, i).wait_recv()
        total = jnp.zeros((BLK, 512), F32)
        for h in range(2 * X):
            total += jnp.dot(
                att[h, i], w[pl.ds(h * 512, 512), :], preferred_element_type=F32
            )
        out[pl.ds(i * BLK, BLK), :] = total.astype(BF16)

    def one_block(i):
        attend(i)
        for n in range(3):
            own(n, i).start()

        @pl.when(i >= 1)
        def _():
            relay_near(i - 1)

    each(0, LB, one_block)

    def rest(i):
        relay_far(i)

        @pl.when(i == 0)
        def _():
            relay_near(LB - 1)

        project(i)

    each(0, LB, rest)

    for d in range(4):
        for kv in range(2):
            hop(kv, d).wait_send()

    def sent_y(d):
        to = lax.rem(y + d, Y)
        col(0, to, y).wait_send()
        col(1, to, y).wait_send()
        each(0, NV, lambda slot: spread(slot, to, y).wait_send())

    def sent_z(d):
        to = lax.rem(z + d, Z)
        to_row(to, z).wait_send()
        along(z, to).wait_send()

    def sent_x(i):
        for n in range(3):
            own(n, i).wait_send()
        for n in range(2):
            forward(n, i).wait_send()
        for n in range(4):
            share(n, i).wait_send()

    each(1, Y, sent_y)
    each(1, Z, sent_z)
    each(0, LB, sent_x)


def body(sizes, queries, keys, values, vertical_blocks, slash_offsets, out_weight):
    Y, Z, X = sizes
    hbm = pl.BlockSpec(memory_space=pltpu.HBM)
    smem = pl.BlockSpec(memory_space=pltpu.SMEM)
    dma = pltpu.SemaphoreType.DMA
    piece = BLK // Y
    return pl.pallas_call(
        functools.partial(kernel, sizes),
        out_shape=jax.ShapeDtypeStruct((ROWS, 512), BF16),
        in_specs=[hbm, hbm, hbm, smem, smem, hbm],
        out_specs=pl.BlockSpec(memory_space=pltpu.VMEM),
        scratch_shapes=[
            pltpu.VMEM((ROWS, 512), BF16),
            pltpu.VMEM(out_weight.shape, BF16),
            pltpu.VMEM((5 * LB, Y, piece, HD), BF16),
            pltpu.VMEM((5 * LB, Y, piece, HD), BF16),
            pltpu.VMEM((2, Y, LB, piece, HD), BF16),
            pltpu.VMEM((NV, 2, piece, HD), BF16),
            pltpu.VMEM((NV, 2, piece, HD), BF16),
            pltpu.VMEM((NV, 2, Y, piece, HD), BF16),
            pltpu.VMEM((GROUP * BLK, HD), BF16),
            pltpu.VMEM((KEYS, HD), BF16),
            pltpu.VMEM((KEYS, 2 * HD), BF16),
            pltpu.VMEM((GROUP * BLK, KEYS), F32),
            pltpu.VMEM((GROUP * BLK, KEYS), BF16),
            pltpu.VMEM((2 * X, LB, BLK, 512), BF16),
            dma((6,)),
            dma((2, 4)),
            dma((2, 4)),
            dma((2, Y)),
            dma((2, Y)),
            dma((Z,)),
            dma((Z,)),
            dma((Z,)),
            dma((Z,)),
            dma((NV, Y)),
            dma((NV, Y)),
            dma((9, LB)),
            dma((4, LB)),
            dma((5, LB)),
        ],
        compiler_params=pltpu.CompilerParams(
            collective_id=0, has_side_effects=True, vmem_limit_bytes=48 * 1024 * 1024
        ),
    )(
        queries,
        keys.reshape(LB, Y, piece, HD),
        values.reshape(LB, Y, piece, HD),
        vertical_blocks,
        slash_offsets,
        out_weight,
    )


def solution(mesh):
    sizes = (8, 8, 4)
    torus = Mesh(mesh.devices.reshape(*sizes, 2), ("y", "z", "x", "core"))
    ctx, heads = ("y", "z"), ("x", "core")
    return jax.shard_map(
        functools.partial(body, sizes),
        mesh=torus,
        in_specs=(
            P(ctx, heads),
            P(ctx, heads),
            P(ctx, heads),
            P(heads, None),
            P(heads, None),
            P(None, heads),
        ),
        out_specs=P(ctx, heads),
        check_vma=False,
    )
```

```python
import functools
import math

import jax
import jax.numpy as jnp
from jax import lax
from jax.experimental import pallas as pl
from jax.experimental.pallas import tpu as pltpu
from jax.sharding import Mesh
from jax.sharding import PartitionSpec as P

HD = 128
BLK = 128
LB = 4
GROUP = 4
NV = 8
NS = 8
ROWS = LB * BLK
HALF = BLK // 2
CHUNKS = ROWS // HALF
KEYS = (NV + NS) * BLK
SCALE = math.log2(math.e) / math.sqrt(HD)
MESH = pl.DeviceIdType.MESH
BF16 = jnp.bfloat16
F32 = jnp.float32


def remote(src, dst, send, recv, where):
    return pltpu.make_async_remote_copy(
        src_ref=src, dst_ref=dst, send_sem=send, recv_sem=recv, device_id=where, device_id_type=MESH
    )


def each(lo, hi, do):
    def step(i, carry):
        do(i)
        return carry

    lax.fori_loop(lo, hi, step, 0)


def kernel(
    sizes,
    q_hbm,
    k_hbm,
    v_hbm,
    vb,
    so,
    w_hbm,
    out,
    q,
    w,
    kall,
    vall,
    thru,
    st1,
    sel,
    st2,
    vert,
    qs,
    ksel,
    vsel,
    s,
    p,
    att,
    outv,
    s_loc,
    s_a,
    r_a,
    s_t,
    r_t,
    s_b1,
    r_b1,
    s_b2,
    r_b2,
    s_b3,
    r_b3,
    s_b4,
    r_b4,
    r_far,
    s_d,
    r_d,
    r_p,
    s_out,
):
    Y, Z, X = sizes
    y, z, x, c = (lax.axis_index(a) for a in ("y", "z", "x", "core"))
    ctx = y * Z + z
    head = x * 2 + c

    def at_y(i):
        return {"y": i}

    def at_z(i):
        return {"z": i}

    right, left = {"x": lax.rem(x + 1, X)}, {"x": lax.rem(x + X - 1, X)}
    other = {"core": 1 - c}

    barrier = pltpu.get_barrier_semaphore()

    def greet(where):
        pl.semaphore_signal(barrier, inc=1, device_id=where, device_id_type=MESH)

    each(1, Y, lambda d: greet(at_y(lax.rem(y + d, Y))))
    each(1, Z, lambda d: greet(at_z(lax.rem(z + d, Z))))
    for where in (right, left, other):
        greet(where)
    pl.semaphore_wait(barrier, Y - 1 + Z - 1 + 3)

    first_z, last_z = z == 0, z == Z - 1
    below = at_y(lax.rem(y + 1, Y))
    beyond = at_z(lax.rem(z + 1, Z))

    def by_last(d, m):
        return d == 1 or (d >= 2 and m < 2)

    def two(ref, at, m):
        return ref.at[pl.ds(at + 2 * (m % 2), 2)]

    def window(d, m):
        return two((kall, vall)[m // 2], LB * d, m)

    def hop(d, m):
        src = two((k_hbm, v_hbm)[m // 2], 0, m) if d == 0 else window(d, m)
        return remote(src, window(d + 1, m), s_a.at[d], r_a.at[d, m], beyond)

    def leg(d, m):
        src = two((k_hbm, v_hbm)[m // 2], 0, m) if d == 0 else window(d, m)
        where = below if by_last(d, m) else beyond
        return remote(src, thru.at[d, m], s_a.at[d], r_t.at[d, m], where)

    def send_hop(d, where, messages=range(4)):
        for send, here in ((hop, jnp.logical_not(last_z)), (leg, last_z)):

            @pl.when(here & where)
            def _():
                for m in messages:
                    if d > 0:
                        hop(d - 1, m).wait_recv()
                    send(d, m).start()

    def relay(d, last):
        @pl.when(last_z if last else first_z)
        def _():
            for m in range(4):
                if by_last(d, m) == last:
                    leg(d, m).wait_recv()
                    remote(
                        thru.at[d, m],
                        window(d + 1, m),
                        s_t.at[d],
                        r_a.at[d, m],
                        beyond if last else below,
                    ).start()

    def left_all(sem, bytes_of):
        remote(bytes_of, bytes_of, sem, r_a.at[0, 0], beyond).wait_send()

    def col(kv, to, frm):
        src = (k_hbm, v_hbm)[kv]
        return remote(src.at[:, to], st1.at[kv, frm], s_b1.at[0], r_b1.at[0], at_y(to))

    def far_first(n, size):
        k = (n + 1) // 2
        return size // 2 + jnp.where(lax.rem(n, 2) == 0, k, -k)

    def send_col(n):
        to = lax.rem(y + far_first(n, Y), Y)
        col(0, to, y).start()
        col(1, to, y).start()

    each(0, Y - 1, send_col)
    send_hop(0, True)
    local = [
        pltpu.make_async_copy(k_hbm.at[:, y], st1.at[0, y], s_loc.at[0]),
        pltpu.make_async_copy(v_hbm.at[:, y], st1.at[1, y], s_loc.at[1]),
        pltpu.make_async_copy(k_hbm, kall.at[pl.ds(0, LB)], s_loc.at[2]),
        pltpu.make_async_copy(v_hbm, vall.at[pl.ds(0, LB)], s_loc.at[3]),
        pltpu.make_async_copy(q_hbm, q, s_loc.at[4]),
        pltpu.make_async_copy(w_hbm, w, s_loc.at[5]),
    ]
    for copy in local:
        copy.start()

    local[0].wait()
    local[1].wait()
    those = st1.at[:, pl.ds(0, Y - 1)]
    remote(those, those, s_b1.at[0], r_b1.at[0], beyond).wait_recv()

    for j in range(NV):
        owner = vb[0, j] // LB
        for kv in range(2):
            sel[j, kv] = st1[kv, owner // Z, lax.rem(vb[0, j], LB)]

    def to_row(to, frm):
        return remote(sel.at[to], st2.at[frm], s_b2.at[0], r_b2.at[0], at_z(to))

    each(0, Z - 1, lambda n: to_row(lax.rem(z + far_first(n, Z), Z), z).start())
    st2[z] = sel[z]

    relay(0, False)
    send_hop(1, z > 0)
    those = st2.at[pl.ds(0, Z - 1)]
    remote(those, those, s_b2.at[0], r_b2.at[0], beyond).wait_recv()

    vert[z, :, y] = st2[lax.rem(vb[0, z] // LB, Z)]

    def along(slot, to):
        here = vert.at[slot, :, y]
        return remote(here, here, s_b3.at[0], r_b3.at[slot], at_z(to))

    def spread(slot, to, frm, send, recv):
        here = vert.at[slot, :, frm]
        return remote(here, here, send, recv, at_y(to))

    def spread_near(slot):
        for n in range(2):
            one, two_on = (lax.rem(y + (k, Y - k)[n], Y) for k in (1, 2))
            spread(slot, two_on, y, s_b4.at[0], r_b4.at[slot, n]).start()
            spread(slot, one, y, s_b4.at[0], r_far.at[0]).start()

    def spread_far(slot):
        for n in range(2):
            frm = lax.rem(y + (Y - 2, 2)[n], Y)
            one, two_on = (lax.rem(y + (k, Y - k)[n], Y) for k in (1, 2))
            spread(slot, y, frm, s_b4.at[0], r_b4.at[slot, n]).wait_recv()

            @pl.when(lax.rem(slot, 2) == n)
            def _():
                spread(slot, two_on, frm, s_b4.at[1], r_far.at[0]).start()

            spread(slot, one, frm, s_b4.at[1], r_far.at[0]).start()

    each(0, Z - 1, lambda n: along(z, lax.rem(z + far_first(n, Z), Z)).start())
    spread_near(z)
    send_hop(2, z >= 2, (0, 1))

    def beside(d):
        return (lax.rem(z + d, Z), lax.rem(z + Z - d, Z))

    def pass_on(d):
        for slot in beside(d):
            along(slot, z).wait_recv()
            spread_near(slot)

        @pl.when(d == 1)
        def _():
            spread_far(z)

        @pl.when(d > 1)
        def _():
            for slot in beside(d - 1):
                spread_far(slot)

    pass_on(1)
    send_hop(2, z >= 2, (2, 3))
    send_hop(1, first_z)
    relay(1, True)
    each(2, Z // 2, pass_on)
    across = lax.rem(z + Z // 2, Z)
    along(across, z).wait_recv()
    spread_near(across)
    relay(2, False)
    send_hop(3, (z >= 3) & (z < Z - 1), (0, 1))
    for slot in beside(Z // 2 - 1):
        spread_far(slot)
    spread_far(across)

    send_hop(3, (z >= 3) & (z < Z - 1), (2, 3))
    send_hop(2, z <= 1)
    relay(2, True)
    send_hop(3, last_z)
    relay(3, False)
    relay(3, True)
    send_hop(3, z < 3)
    for copy in local[2:]:
        copy.wait()

    those = vert.at[pl.ds(0, 5)]
    remote(those, those, s_b4.at[0], r_far.at[0], beyond).wait_recv()

    for m in range(4):
        hop(3, m).wait_recv()

    zero_at = 0
    for j in range(NS):
        zero_at += jnp.where(so[0, j] == 0, j, 0)
    ones = jnp.ones((BLK, HD), F32)

    def put(slot, valid, key, value, first):
        rows = pl.ds(slot * BLK, BLK)
        kept = jnp.where(valid, 1.0, 0.0)
        key = key.reshape(BLK, HD).astype(F32)
        value = value.reshape(BLK, HD).astype(F32)
        if first is not None:
            key = key * kept + first * (1.0 - kept)
            value = value * kept
        ksel[rows, :] = key.astype(BF16)
        vsel[rows, pl.ds(0, HD)] = value.astype(BF16)
        vsel[rows, pl.ds(HD, HD)] = (ones * kept).astype(BF16)
        return key

    def select(i):
        block = ctx * LB + i
        key = put(0, True, kall[i], vall[i], None)
        first = jnp.broadcast_to(key[0:1, :], (BLK, HD))
        for j in range(NS - 1):
            off = so[0, j + jnp.where(zero_at <= j, 1, 0)]
            back = (off - i + LB - 1) // LB
            at = LB * back + (i - off + LB * back)
            put(1 + j, block - off >= 0, kall[at], vall[at], first)
        for j in range(NV):
            seen = vb[0, j]
            valid = seen < block
            for o in range(NS):
                valid = valid & (seen != block - so[0, o])
            put(NS + j, valid, vert[j, 0], vert[j, 1], first)

    def attend(n):
        for g in range(GROUP):
            qs[pl.ds(g * HALF, HALF), :] = q[pl.ds(n * HALF, HALF), pl.ds(g * HD, HD)]
        top = None
        for j in range(KEYS // 256):
            cols = pl.ds(j * 256, 256)
            part = lax.dot_general(
                qs[...], ksel[cols, :], (((1,), (1,)), ((), ())), preferred_element_type=F32
            )
            if j == 0:
                row = lax.rem(lax.broadcasted_iota(jnp.int32, part.shape, 0), HALF)
                row += lax.rem(n, 2) * HALF
                col_at = lax.broadcasted_iota(jnp.int32, part.shape, 1)
                part = jnp.where((col_at <= row) | (col_at >= BLK), part, -1e30)
            s[:, cols] = part
            two = jnp.maximum(part[:, :HD], part[:, HD:])
            top = two if top is None else jnp.maximum(top, two)
        top = jnp.max(top, axis=1, keepdims=True)
        for j in range(KEYS // 256):
            cols = pl.ds(j * 256, 256)
            p[:, cols] = jnp.exp2((s[:, cols] - top) * SCALE).astype(BF16)
        total = jnp.dot(p[...], vsel[...], preferred_element_type=F32)
        total = (total[:, :HD] / total[:, HD:]).astype(BF16)
        for g in range(GROUP):
            att[head, n, :, pl.ds(g * HD, HD)] = total[g * HALF : (g + 1) * HALF, :]

    def own(m, n):
        here = att.at[head, n]
        where = (right, left, other)[m]
        recv = r_p.at[n // 2] if m == 2 else r_d.at[m, n]
        return remote(here, here, s_d.at[m], recv, where)

    def chunk(m, n):
        return att.at[lax.rem(x + (X - 1, 1, 2)[m], X) * 2 + c, n]

    def got(m, n):
        here = chunk(m, n)
        return remote(here, here, s_d.at[0], r_d.at[m, n], right)

    def share(m, n):
        here = chunk(m, n)
        return remote(here, here, s_d.at[4 + m], r_p.at[n // 2], other)

    def relay_near(n):
        for m in range(2):
            got(m, n).wait_recv()

            @pl.when(lax.rem(n, 2) == m)
            def _():
                here = chunk(m, n)
                remote(here, here, s_d.at[3], r_d.at[2, n], (right, left)[m]).start()

            share(m, n).start()

    def relay_far(n):
        got(2, n).wait_recv()
        share(2, n).start()

    def result(i):
        rows = pl.ds(i * BLK, BLK)
        return pltpu.make_async_copy(outv.at[rows], out.at[rows], s_out.at[i])

    def project(i):
        remote(att.at[0], att.at[0], s_d.at[0], r_p.at[i], other).wait_recv()
        total = jnp.zeros((BLK, 512), F32)
        for h in range(2 * X):
            rows = att[h, pl.ds(2 * i, 2)].reshape(BLK, 512)
            total += jnp.dot(rows, w[pl.ds(h * 512, 512), :], preferred_element_type=F32)
        outv[pl.ds(i * BLK, BLK), :] = total.astype(BF16)
        result(i).start()

    def one_chunk(n):
        @pl.when(lax.rem(n, 2) == 0)
        def _():
            select(n // 2)

        attend(n)
        for m in range(3):
            own(m, n).start()

        @pl.when(n >= 3)
        def _():
            relay_near(n - 3)

    each(0, CHUNKS, one_chunk)

    def sent_early():
        left_all(s_b1.at[0], st1.at[:, pl.ds(0, Y - 1)])
        left_all(s_b2.at[0], st2.at[pl.ds(0, Z - 1)])
        left_all(s_b3.at[0], st2.at[pl.ds(0, Z - 1)])
        left_all(s_b4.at[0], vert.at[pl.ds(0, 4)])
        left_all(s_b4.at[1], vert.at[pl.ds(0, 3)])
        for d in range(4):
            left_all(s_a.at[d], thru.at[0])
        for last in (True, False):

            @pl.when(last_z if last else first_z)
            def _():
                for d in range(4):
                    n = sum(by_last(d, m) == last for m in range(4))
                    if n:
                        left_all(s_t.at[d], thru.at[d, pl.ds(0, n)])

    sent_early()
    each(0, 3, relay_far)
    relay_near(5)
    relay_far(3)
    relay_near(6)

    def rest(i):
        @pl.when(i == 1)
        def _():
            relay_near(7)

        @pl.when(i >= 1)
        def _():
            relay_far(4 + i - 1)

        @pl.when(i == 3)
        def _():
            relay_far(7)

        project(i)

    each(0, LB, rest)

    for m in range(7):
        left_all(s_d.at[m], att.at[0])
    for i in range(LB):
        result(i).wait()


def body(sizes, queries, keys, values, vertical_blocks, slash_offsets, out_weight):
    Y, Z, X = sizes
    hbm = pl.BlockSpec(memory_space=pltpu.HBM)
    smem = pl.BlockSpec(memory_space=pltpu.SMEM)
    dma = pltpu.SemaphoreType.DMA
    piece = BLK // Y
    return pl.pallas_call(
        functools.partial(kernel, sizes),
        out_shape=jax.ShapeDtypeStruct((ROWS, 512), BF16),
        in_specs=[hbm, hbm, hbm, smem, smem, hbm],
        out_specs=hbm,
        scratch_shapes=[
            pltpu.VMEM((ROWS, 512), BF16),
            pltpu.VMEM(out_weight.shape, BF16),
            pltpu.VMEM((5 * LB, Y, piece, HD), BF16),
            pltpu.VMEM((5 * LB, Y, piece, HD), BF16),
            pltpu.VMEM((4, 4, 2, Y, piece, HD), BF16),
            pltpu.VMEM((2, Y, LB, piece, HD), BF16),
            pltpu.VMEM((NV, 2, piece, HD), BF16),
            pltpu.VMEM((NV, 2, piece, HD), BF16),
            pltpu.VMEM((NV, 2, Y, piece, HD), BF16),
            pltpu.VMEM((GROUP * HALF, HD), BF16),
            pltpu.VMEM((KEYS, HD), BF16),
            pltpu.VMEM((KEYS, 2 * HD), BF16),
            pltpu.VMEM((GROUP * HALF, KEYS), F32),
            pltpu.VMEM((GROUP * HALF, KEYS), BF16),
            pltpu.VMEM((2 * X, CHUNKS, HALF, 512), BF16),
            pltpu.VMEM((ROWS, 512), BF16),
            dma((6,)),
            dma((4,)),
            dma((4, 4)),
            dma((4,)),
            dma((4, 4)),
            dma((1,)),
            dma((1,)),
            dma((1,)),
            dma((1,)),
            dma((1,)),
            dma((NV,)),
            dma((2,)),
            dma((NV, 2)),
            dma((1,)),
            dma((7,)),
            dma((3, CHUNKS)),
            dma((LB,)),
            dma((LB,)),
        ],
        compiler_params=pltpu.CompilerParams(
            collective_id=0, has_side_effects=True, vmem_limit_bytes=67_043_328
        ),
    )(
        queries,
        keys.reshape(LB, Y, piece, HD),
        values.reshape(LB, Y, piece, HD),
        vertical_blocks,
        slash_offsets,
        out_weight,
    )


def solution(mesh):
    sizes = (8, 8, 4)
    torus = Mesh(mesh.devices.reshape(*sizes, 2), ("y", "z", "x", "core"))
    ctx, heads = ("y", "z"), ("x", "core")
    return jax.shard_map(
        functools.partial(body, sizes),
        mesh=torus,
        in_specs=(
            P(ctx, heads),
            P(ctx, heads),
            P(ctx, heads),
            P(heads, None),
            P(heads, None),
            P(None, heads),
        ),
        out_specs=P(ctx, heads),
        check_vma=False,
    )
```

```python
import functools
import math

import jax
import jax.numpy as jnp
from jax import lax
from jax.experimental import pallas as pl
from jax.experimental.pallas import tpu as pltpu
from jax.sharding import Mesh
from jax.sharding import PartitionSpec as P

HD = 128
BLK = 128
LB = 4
GROUP = 4
NV = 8
NS = 8
ROWS = LB * BLK
HALF = BLK // 2
CHUNKS = ROWS // HALF
KEYS = (NV + NS) * BLK
SCALE = math.log2(math.e) / math.sqrt(HD)
MESH = pl.DeviceIdType.MESH
BF16 = jnp.bfloat16
F32 = jnp.float32


def remote(src, dst, send, recv, where):
    return pltpu.make_async_remote_copy(
        src_ref=src, dst_ref=dst, send_sem=send, recv_sem=recv, device_id=where, device_id_type=MESH
    )


def each(lo, hi, do):
    def step(i, carry):
        do(i)
        return carry

    lax.fori_loop(lo, hi, step, 0)


def kernel(
    sizes,
    q_hbm,
    k_hbm,
    v_hbm,
    vb,
    so,
    w_hbm,
    out,
    q,
    w,
    kall,
    vall,
    rest,
    thru,
    st1,
    sel,
    st2,
    vert,
    qs,
    ksel,
    vsel,
    s,
    p,
    att,
    outv,
    s_loc,
    s_a,
    r_a,
    s_t,
    r_t,
    s_b1,
    r_b1,
    s_b2,
    r_b2,
    s_b3,
    r_b3,
    s_b4,
    r_b4,
    r_far,
    s_d,
    r_d,
    r_p,
    s_out,
):
    Y, Z, X = sizes
    y, z, x, c = (lax.axis_index(a) for a in ("y", "z", "x", "core"))
    ctx = y * Z + z
    head = x * 2 + c

    def at_y(i):
        return {"y": i}

    def at_z(i):
        return {"z": i}

    right, left = {"x": lax.rem(x + 1, X)}, {"x": lax.rem(x + X - 1, X)}
    other = {"core": 1 - c}

    barrier = pltpu.get_barrier_semaphore()

    def greet(where):
        pl.semaphore_signal(barrier, inc=1, device_id=where, device_id_type=MESH)

    each(1, Y, lambda d: greet(at_y(lax.rem(y + d, Y))))
    each(1, Z, lambda d: greet(at_z(lax.rem(z + d, Z))))
    for where in (right, left, other):
        greet(where)
    pl.semaphore_wait(barrier, Y - 1 + Z - 1 + 3)

    LATE, EARLY = (1, 3), (0, 2)
    first_z, last_z = z == 0, z == Z - 1
    below = at_y(lax.rem(y + 1, Y))
    beyond = at_z(lax.rem(z + 1, Z))

    def by_last(d, m):
        return d >= 1 and m % 2 == 1

    def two(ref, at, m):
        return ref.at[pl.ds(at + 2 * (m % 2), 2)]

    def window(d, m):
        if d == 4 and m in EARLY:
            return rest.at[m // 2]
        return two((kall, vall)[m // 2], LB * d, m)

    def hop(d, m):
        src = two((k_hbm, v_hbm)[m // 2], 0, m) if d == 0 else window(d, m)
        return remote(src, window(d + 1, m), s_a.at[d], r_a.at[d, m], beyond)

    def leg(d, m):
        src = two((k_hbm, v_hbm)[m // 2], 0, m) if d == 0 else window(d, m)
        where = below if by_last(d, m) else beyond
        return remote(src, thru.at[d, m], s_a.at[d], r_t.at[d, m], where)

    def send_hop(d, where, messages=LATE + EARLY):
        for send, here in ((hop, jnp.logical_not(last_z)), (leg, last_z)):

            @pl.when(here & where)
            def _():
                for m in messages:
                    if d > 0:
                        hop(d - 1, m).wait_recv()
                    send(d, m).start()

    def relay(d, last, messages=LATE + EARLY):
        @pl.when(last_z if last else first_z)
        def _():
            for m in messages:
                if by_last(d, m) == last:
                    leg(d, m).wait_recv()
                    remote(
                        thru.at[d, m],
                        window(d + 1, m),
                        s_t.at[d],
                        r_a.at[d, m],
                        beyond if last else below,
                    ).start()

    def left_all(sem, bytes_of):
        remote(bytes_of, bytes_of, sem, r_a.at[0, 0], beyond).wait_send()

    def col(kv, to, frm):
        src = (k_hbm, v_hbm)[kv]
        return remote(src.at[:, to], st1.at[kv, frm], s_b1.at[0], r_b1.at[0], at_y(to))

    def far_first(n, size):
        k = (n + 1) // 2
        return size // 2 + jnp.where(lax.rem(n, 2) == 0, k, -k)

    def send_col(n):
        to = lax.rem(y + far_first(n, Y), Y)
        col(0, to, y).start()
        col(1, to, y).start()

    each(0, Y - 1, send_col)
    send_hop(0, True)
    local = [
        pltpu.make_async_copy(k_hbm.at[:, y], st1.at[0, y], s_loc.at[0]),
        pltpu.make_async_copy(v_hbm.at[:, y], st1.at[1, y], s_loc.at[1]),
        pltpu.make_async_copy(k_hbm, kall.at[pl.ds(0, LB)], s_loc.at[2]),
        pltpu.make_async_copy(v_hbm, vall.at[pl.ds(0, LB)], s_loc.at[3]),
        pltpu.make_async_copy(q_hbm, q, s_loc.at[4]),
        pltpu.make_async_copy(w_hbm, w, s_loc.at[5]),
    ]
    for copy in local:
        copy.start()

    relay(0, False, LATE)
    send_hop(1, z > 0, LATE)
    local[0].wait()
    local[1].wait()
    those = st1.at[:, pl.ds(0, Y - 1)]
    remote(those, those, s_b1.at[0], r_b1.at[0], beyond).wait_recv()

    for j in range(NV):
        owner = vb[0, j] // LB
        for kv in range(2):
            sel[j, kv] = st1[kv, owner // Z, lax.rem(vb[0, j], LB)]

    def to_row(to, frm):
        return remote(sel.at[to], st2.at[frm], s_b2.at[0], r_b2.at[0], at_z(to))

    each(0, Z - 1, lambda n: to_row(lax.rem(z + far_first(n, Z), Z), z).start())
    st2[z] = sel[z]

    relay(0, False, EARLY)
    send_hop(1, z > 0, EARLY)
    those = st2.at[pl.ds(0, Z - 1)]
    remote(those, those, s_b2.at[0], r_b2.at[0], beyond).wait_recv()

    vert[z, :, y] = st2[lax.rem(vb[0, z] // LB, Z)]

    def along(slot, to):
        here = vert.at[slot, :, y]
        return remote(here, here, s_b3.at[0], r_b3.at[slot], at_z(to))

    def spread(slot, to, frm, send, recv):
        here = vert.at[slot, :, frm]
        return remote(here, here, send, recv, at_y(to))

    def spread_near(slot):
        for n in range(2):
            one, two_on = (lax.rem(y + (k, Y - k)[n], Y) for k in (1, 2))
            spread(slot, two_on, y, s_b4.at[0], r_b4.at[slot, n]).start()
            spread(slot, one, y, s_b4.at[0], r_far.at[0]).start()

    def spread_far(slot):
        for n in range(2):
            frm = lax.rem(y + (Y - 2, 2)[n], Y)
            one, two_on = (lax.rem(y + (k, Y - k)[n], Y) for k in (1, 2))
            spread(slot, y, frm, s_b4.at[0], r_b4.at[slot, n]).wait_recv()

            @pl.when(lax.rem(slot, 2) == n)
            def _():
                spread(slot, two_on, frm, s_b4.at[1], r_far.at[0]).start()

            spread(slot, one, frm, s_b4.at[1], r_far.at[0]).start()

    each(0, Z - 1, lambda n: along(z, lax.rem(z + far_first(n, Z), Z)).start())
    spread_near(z)
    send_hop(2, z >= 2)
    relay(1, True)
    relay(1, False)
    send_hop(1, first_z, LATE)

    def beside(d):
        return (lax.rem(z + d, Z), lax.rem(z + Z - d, Z))

    def pass_on(d):
        for slot in beside(d):
            along(slot, z).wait_recv()
            spread_near(slot)

    def spread_both(d):
        for slot in beside(d):
            spread_far(slot)

    pass_on(1)
    send_hop(1, first_z, EARLY)
    pass_on(2)
    spread_far(z)
    pass_on(3)
    across = lax.rem(z + Z // 2, Z)
    along(across, z).wait_recv()
    spread_near(across)
    relay(2, True)
    send_hop(2, z < 2, LATE)
    send_hop(3, z >= 3, LATE)
    relay(2, False)
    send_hop(2, z < 2, EARLY)
    each(1, 3, spread_both)
    send_hop(3, z >= 3, EARLY)
    send_hop(3, z < 2, LATE)
    spread_both(3)
    spread_far(across)
    send_hop(3, z == 2, LATE)
    relay(3, True)
    relay(3, False, (0,))
    send_hop(3, z < 3, EARLY)
    relay(3, False, (2,))
    for copy in local[2:]:
        copy.wait()

    those = vert.at[pl.ds(0, 5)]
    remote(those, those, s_b4.at[0], r_far.at[0], beyond).wait_recv()

    for m in LATE:
        hop(3, m).wait_recv()

    zero_at = 0
    for j in range(NS):
        zero_at += jnp.where(so[0, j] == 0, j, 0)
    ones = jnp.ones((BLK, HD), F32)

    def put(slot, valid, key, value, first):
        rows = pl.ds(slot * BLK, BLK)
        kept = jnp.where(valid, 1.0, 0.0)
        key = key.reshape(BLK, HD).astype(F32)
        value = value.reshape(BLK, HD).astype(F32)
        if first is not None:
            key = key * kept + first * (1.0 - kept)
            value = value * kept
        ksel[rows, :] = key.astype(BF16)
        vsel[rows, pl.ds(0, HD)] = value.astype(BF16)
        vsel[rows, pl.ds(HD, HD)] = (ones * kept).astype(BF16)
        return key

    def select(i):
        block = ctx * LB + i
        key = put(0, True, kall[i], vall[i], None)
        first = jnp.broadcast_to(key[0:1, :], (BLK, HD))
        for j in range(NS - 1):
            off = so[0, j + jnp.where(zero_at <= j, 1, 0)]
            back = (off - i + LB - 1) // LB
            at = LB * back + (i - off + LB * back)
            put(1 + j, block - off >= 0, kall[at], vall[at], first)
        for j in range(NV):
            seen = vb[0, j]
            valid = seen < block
            for o in range(NS):
                valid = valid & (seen != block - so[0, o])
            put(NS + j, valid, vert[j, 0], vert[j, 1], first)

    def block_of(n):
        return LB - 1 - n // 2

    def attend(n):
        for g in range(GROUP):
            rows = pl.ds(block_of(n) * BLK + lax.rem(n, 2) * HALF, HALF)
            qs[pl.ds(g * HALF, HALF), :] = q[rows, pl.ds(g * HD, HD)]
        top = None
        for j in range(KEYS // 256):
            cols = pl.ds(j * 256, 256)
            part = lax.dot_general(
                qs[...], ksel[cols, :], (((1,), (1,)), ((), ())), preferred_element_type=F32
            )
            if j == 0:
                row = lax.rem(lax.broadcasted_iota(jnp.int32, part.shape, 0), HALF)
                row += lax.rem(n, 2) * HALF
                col_at = lax.broadcasted_iota(jnp.int32, part.shape, 1)
                part = jnp.where((col_at <= row) | (col_at >= BLK), part, -1e30)
            s[:, cols] = part
            two = jnp.maximum(part[:, :HD], part[:, HD:])
            top = two if top is None else jnp.maximum(top, two)
        top = jnp.max(top, axis=1, keepdims=True)
        for j in range(KEYS // 256):
            cols = pl.ds(j * 256, 256)
            p[:, cols] = jnp.exp2((s[:, cols] - top) * SCALE).astype(BF16)
        total = jnp.dot(p[...], vsel[...], preferred_element_type=F32)
        total = (total[:, :HD] / total[:, HD:]).astype(BF16)
        for g in range(GROUP):
            att[head, n, :, pl.ds(g * HD, HD)] = total[g * HALF : (g + 1) * HALF, :]

    part = HALF // 2

    def own(m, n):
        here = att.at[head, n]
        where = (right, left, other)[m]
        recv = r_p.at[n // 2] if m == 2 else r_d.at[m, n]
        return remote(here, here, s_d.at[m], recv, where)

    def chunk(m, n):
        return att.at[lax.rem(x + (X - 1, 1, 2)[m], X) * 2 + c, n]

    def got(m, n):
        here = chunk(m, n)
        return remote(here, here, s_d.at[0], r_d.at[m, n], right)

    def share(m, n):
        here = chunk(m, n)
        return remote(here, here, s_d.at[4 + m], r_p.at[n // 2], other)

    def relay_near(n, split=False):
        for m in range(2):
            got(m, n).wait_recv()
            if split:
                here = chunk(m, n).at[pl.ds((0, part)[m], part)]
                remote(here, here, s_d.at[3], r_d.at[2, n], (right, left)[m]).start()
            else:

                @pl.when(lax.rem(n, 2) == m)
                def _():
                    here = chunk(m, n)
                    remote(here, here, s_d.at[3], r_d.at[2, n], (right, left)[m]).start()

            share(m, n).start()

    def relay_far(n):
        got(2, n).wait_recv()
        share(2, n).start()

    def result(i):
        rows = pl.ds((LB - 1 - i) * BLK, BLK)
        return pltpu.make_async_copy(outv.at[rows], out.at[rows], s_out.at[i])

    def project(i):
        remote(att.at[0], att.at[0], s_d.at[0], r_p.at[i], other).wait_recv()
        total = jnp.zeros((BLK, 512), F32)
        for h in range(2 * X):
            rows = att[h, pl.ds(2 * i, 2)].reshape(BLK, 512)
            total += jnp.dot(rows, w[pl.ds(h * 512, 512), :], preferred_element_type=F32)
        outv[pl.ds((LB - 1 - i) * BLK, BLK), :] = total.astype(BF16)
        result(i).start()

    def one_chunk(n):
        @pl.when(n == CHUNKS // 2)
        def _():
            for m in EARLY:
                hop(3, m).wait_recv()
                (kall, vall)[m // 2][pl.ds(LB * 4, 2)] = rest[m // 2]

        @pl.when(lax.rem(n, 2) == 0)
        def _():
            select(block_of(n))

        attend(n)
        for m in range(3):
            own(m, n).start()

        @pl.when(n >= 3)
        def _():
            relay_near(n - 3)

    each(0, CHUNKS, one_chunk)

    def sent_early():
        left_all(s_b1.at[0], st1.at[:, pl.ds(0, Y - 1)])
        left_all(s_b2.at[0], st2.at[pl.ds(0, Z - 1)])
        left_all(s_b3.at[0], st2.at[pl.ds(0, Z - 1)])
        left_all(s_b4.at[0], vert.at[pl.ds(0, 4)])
        left_all(s_b4.at[1], vert.at[pl.ds(0, 3)])
        for d in range(4):
            left_all(s_a.at[d], thru.at[0])
        for last in (True, False):

            @pl.when(last_z if last else first_z)
            def _():
                for d in range(4):
                    n = sum(by_last(d, m) == last for m in range(4))
                    if n:
                        left_all(s_t.at[d], thru.at[d, pl.ds(0, n)])

    sent_early()
    each(0, 3, relay_far)
    relay_near(5)
    relay_far(3)
    relay_near(6)
    relay_near(CHUNKS - 1, split=True)
    project(0)
    relay_far(4)
    relay_far(5)
    project(1)
    relay_far(6)
    relay_far(7)
    project(2)
    project(3)
    for m in range(7):
        left_all(s_d.at[m], att.at[0])
    for i in range(LB):
        result(i).wait()


def body(sizes, queries, keys, values, vertical_blocks, slash_offsets, out_weight):
    Y, Z, X = sizes
    hbm = pl.BlockSpec(memory_space=pltpu.HBM)
    smem = pl.BlockSpec(memory_space=pltpu.SMEM)
    dma = pltpu.SemaphoreType.DMA
    piece = BLK // Y
    return pl.pallas_call(
        functools.partial(kernel, sizes),
        out_shape=jax.ShapeDtypeStruct((ROWS, 512), BF16),
        in_specs=[hbm, hbm, hbm, smem, smem, hbm],
        out_specs=hbm,
        scratch_shapes=[
            pltpu.VMEM((ROWS, 512), BF16),
            pltpu.VMEM(out_weight.shape, BF16),
            pltpu.VMEM((5 * LB, Y, piece, HD), BF16),
            pltpu.VMEM((5 * LB, Y, piece, HD), BF16),
            pltpu.VMEM((2, 2, Y, piece, HD), BF16),
            pltpu.VMEM((4, 4, 2, Y, piece, HD), BF16),
            pltpu.VMEM((2, Y, LB, piece, HD), BF16),
            pltpu.VMEM((NV, 2, piece, HD), BF16),
            pltpu.VMEM((NV, 2, piece, HD), BF16),
            pltpu.VMEM((NV, 2, Y, piece, HD), BF16),
            pltpu.VMEM((GROUP * HALF, HD), BF16),
            pltpu.VMEM((KEYS, HD), BF16),
            pltpu.VMEM((KEYS, 2 * HD), BF16),
            pltpu.VMEM((GROUP * HALF, KEYS), F32),
            pltpu.VMEM((GROUP * HALF, KEYS), BF16),
            pltpu.VMEM((2 * X, CHUNKS, HALF, 512), BF16),
            pltpu.VMEM((ROWS, 512), BF16),
            dma((6,)),
            dma((4,)),
            dma((4, 4)),
            dma((4,)),
            dma((4, 4)),
            dma((1,)),
            dma((1,)),
            dma((1,)),
            dma((1,)),
            dma((1,)),
            dma((NV,)),
            dma((2,)),
            dma((NV, 2)),
            dma((1,)),
            dma((7,)),
            dma((3, CHUNKS)),
            dma((LB,)),
            dma((LB,)),
        ],
        compiler_params=pltpu.CompilerParams(
            collective_id=0, has_side_effects=True, vmem_limit_bytes=67_043_328
        ),
    )(
        queries,
        keys.reshape(LB, Y, piece, HD),
        values.reshape(LB, Y, piece, HD),
        vertical_blocks,
        slash_offsets,
        out_weight,
    )


def solution(mesh):
    sizes = (8, 8, 4)
    torus = Mesh(mesh.devices.reshape(*sizes, 2), ("y", "z", "x", "core"))
    ctx, heads = ("y", "z"), ("x", "core")
    return jax.shard_map(
        functools.partial(body, sizes),
        mesh=torus,
        in_specs=(
            P(ctx, heads),
            P(ctx, heads),
            P(ctx, heads),
            P(heads, None),
            P(heads, None),
            P(None, heads),
        ),
        out_specs=P(ctx, heads),
        check_vma=False,
    )
```

```python
import functools
import math

import jax
import jax.numpy as jnp
from jax import lax
from jax.experimental import pallas as pl
from jax.experimental.pallas import tpu as pltpu
from jax.sharding import Mesh
from jax.sharding import PartitionSpec as P

HD = 128
BLK = 128
LB = 4
GROUP = 4
NV = 8
NS = 8
ROWS = LB * BLK
HALF = BLK // 2
CHUNKS = ROWS // HALF
KEYS = (NV + NS) * BLK
SCALE = math.log2(math.e) / math.sqrt(HD)
MESH = pl.DeviceIdType.MESH
BF16 = jnp.bfloat16
F32 = jnp.float32


def remote(src, dst, send, recv, where):
    return pltpu.make_async_remote_copy(
        src_ref=src, dst_ref=dst, send_sem=send, recv_sem=recv, device_id=where, device_id_type=MESH
    )


def each(lo, hi, do):
    def step(i, carry):
        do(i)
        return carry

    lax.fori_loop(lo, hi, step, 0)


def kernel(
    sizes,
    q_hbm,
    k_hbm,
    v_hbm,
    vb_hbm,
    so_hbm,
    w_hbm,
    out,
    q,
    w,
    kall,
    vall,
    rest,
    thru,
    st1,
    sel,
    st2,
    vert,
    qs,
    ksel,
    vsel,
    s,
    p,
    att,
    vb,
    so,
    s_loc,
    s_early,
    r_a,
    r_t,
    r_b1,
    r_b2,
    r_b3,
    r_b4,
    r_far,
    s_d,
    r_d,
    r_p,
):
    Y, Z, X = sizes
    y, z, x, c = (lax.axis_index(a) for a in ("y", "z", "x", "core"))
    ctx = y * Z + z
    head = x * 2 + c

    def at_y(i):
        return {"y": i}

    def at_z(i):
        return {"z": i}

    right, left = {"x": lax.rem(x + 1, X)}, {"x": lax.rem(x + X - 1, X)}
    other = {"core": 1 - c}

    tables = [
        pltpu.make_async_copy(vb_hbm, vb, s_loc.at[4]),
        pltpu.make_async_copy(so_hbm, so, s_loc.at[5]),
    ]
    for table in tables:
        table.start()
    barrier = pltpu.get_barrier_semaphore()

    def greet(where):
        pl.semaphore_signal(barrier, inc=1, device_id=where, device_id_type=MESH)

    each(1, Y, lambda d: greet(at_y(lax.rem(y + d, Y))))
    each(1, Z, lambda d: greet(at_z(lax.rem(z + d, Z))))
    for where in (right, left, other):
        greet(where)
    pl.semaphore_wait(barrier, Y - 1 + Z - 1 + 3)

    EARLY, LATE = 0, 1
    first_z, last_z = z == 0, z == Z - 1
    below = at_y(lax.rem(y + 1, Y))
    beyond = at_z(lax.rem(z + 1, Z))

    def by_last(d, half):
        return d >= 1 and half == LATE

    def window(d, kv, half):
        if d == 4 and half == EARLY:
            return rest.at[kv]
        return (kall, vall)[kv].at[pl.ds(LB * d + 2 * half, 2)]

    def source(d, kv, half):
        return (k_hbm, v_hbm)[kv].at[pl.ds(2 * half, 2)] if d == 0 else window(d, kv, half)

    def came(sem, bytes_of):
        remote(bytes_of, bytes_of, s_early.at[0], sem, beyond).wait_recv()

    def send_hop(d, where, halves=(LATE, EARLY)):
        for last, here in ((False, jnp.logical_not(last_z)), (True, last_z)):

            @pl.when(here & where)
            def _():
                for half in halves:
                    if d > 0:
                        came(r_a.at[d - 1, half], kall.at[pl.ds(0, LB)])
                    for kv in range(2):
                        to, recv = window(d + 1, kv, half), r_a.at[d, half]
                        if last:
                            to, recv = thru.at[d, kv, half], r_t.at[d, half]
                        target = below if last and by_last(d, half) else beyond
                        remote(source(d, kv, half), to, s_early.at[0], recv, target).start()

    def relay(d, last, halves=(LATE, EARLY)):
        @pl.when(last_z if last else first_z)
        def _():
            for half in halves:
                if by_last(d, half) == last:
                    came(r_t.at[d, half], kall.at[pl.ds(0, LB)])
                    for kv in range(2):
                        remote(
                            thru.at[d, kv, half],
                            window(d + 1, kv, half),
                            s_early.at[0],
                            r_a.at[d, half],
                            beyond if last else below,
                        ).start()

    def left_all(sem, bytes_of):
        remote(bytes_of, bytes_of, sem, r_a.at[0, 0], beyond).wait_send()

    def col(kv, to, frm):
        src = (k_hbm, v_hbm)[kv]
        return remote(src.at[:, to], st1.at[kv, frm], s_early.at[0], r_b1.at[0], at_y(to))

    def far_first(n, size):
        k = (n + 1) // 2
        return size // 2 + jnp.where(lax.rem(n, 2) == 0, k, -k)

    def send_col(n):
        to = lax.rem(y + far_first(n, Y), Y)
        col(0, to, y).start()
        col(1, to, y).start()

    each(0, Y - 1, send_col)
    send_hop(0, True)
    for src, to, sem in (
        (k_hbm.at[:, y], st1.at[0, y], 0),
        (v_hbm.at[:, y], st1.at[1, y], 0),
        (k_hbm, kall.at[pl.ds(0, LB)], 1),
        (v_hbm, vall.at[pl.ds(0, LB)], 1),
        (q_hbm, q, 2),
        (w_hbm, w, 3),
    ):
        pltpu.make_async_copy(src, to, s_loc.at[sem]).start()

    relay(0, False, (LATE,))
    send_hop(1, z > 0, (LATE,))
    pltpu.make_async_copy(st1.at[:, 0], st1.at[:, 0], s_loc.at[0]).wait()
    came(r_b1.at[0], st1.at[:, pl.ds(0, Y - 1)])

    for table in tables:
        table.wait()
    for j in range(NV):
        owner = vb[0, j] // LB
        for kv in range(2):
            sel[j, kv] = st1[kv, owner // Z, lax.rem(vb[0, j], LB)]

    def to_row(to, frm):
        return remote(sel.at[to], st2.at[frm], s_early.at[0], r_b2.at[0], at_z(to))

    each(0, Z - 1, lambda n: to_row(lax.rem(z + far_first(n, Z), Z), z).start())
    st2[z] = sel[z]

    relay(0, False, (EARLY,))
    send_hop(1, z > 0, (EARLY,))
    came(r_b2.at[0], st2.at[pl.ds(0, Z - 1)])

    vert[z, :, y] = st2[lax.rem(vb[0, z] // LB, Z)]

    def along(d):
        here = vert.at[z, :, y]
        to = at_z(lax.rem(z + d, Z))
        remote(here, here, s_early.at[0], r_b3.at[jnp.minimum(d, Z - d)], to).start()

    def spread(slot, to, frm, recv):
        here = vert.at[slot, :, frm]
        remote(here, here, s_early.at[0], recv, at_y(to)).start()

    def beside(d):
        if isinstance(d, int) and d in (0, Z // 2):
            return (lax.rem(z + d, Z),)
        return (lax.rem(z + d, Z), lax.rem(z + Z - d, Z))

    def spread_near(d):
        for slot in beside(d):
            for n in range(2):
                one, two = (lax.rem(y + (k, Y - k)[n], Y) for k in (1, 2))
                spread(slot, two, y, r_b4.at[d])
                spread(slot, one, y, r_far.at[0])

    def spread_far(d):
        came(r_b4.at[d], st2.at[pl.ds(0, 2 * len(beside(d)))])
        for slot in beside(d):
            for n in range(2):
                frm = lax.rem(y + (Y - 2, 2)[n], Y)
                one, two = (lax.rem(y + (k, Y - k)[n], Y) for k in (1, 2))

                @pl.when(lax.rem(slot, 2) == n)
                def _():
                    spread(slot, two, frm, r_far.at[0])

                spread(slot, one, frm, r_far.at[0])

    def pass_on(d):
        came(r_b3.at[d], st2.at[pl.ds(0, len(beside(d)))])
        spread_near(d)

    each(0, Z - 1, lambda n: along(far_first(n, Z)))
    spread_near(0)
    send_hop(1, first_z, (LATE,))
    relay(1, True)
    relay(1, False)
    send_hop(2, z >= 2)

    pass_on(1)
    send_hop(1, first_z, (EARLY,))
    pass_on(2)
    spread_far(0)
    pass_on(3)
    pass_on(4)
    send_hop(2, z < 2, (LATE,))
    send_hop(3, z >= 3, (LATE,))
    relay(2, True)
    relay(2, False)
    send_hop(2, z < 2, (EARLY,))
    spread_far(1)
    spread_far(2)
    send_hop(3, z >= 3, (EARLY,))
    send_hop(3, z < 2, (LATE,))
    spread_far(3)
    spread_far(4)
    send_hop(3, z == 2, (LATE,))
    relay(3, True)
    send_hop(3, z < 3, (EARLY,))
    pltpu.make_async_copy(thru.at[0], thru.at[0], s_loc.at[1]).wait()
    pltpu.make_async_copy(q_hbm, q, s_loc.at[2]).wait()
    pltpu.make_async_copy(w_hbm, w, s_loc.at[3]).wait()

    came(r_far.at[0], vert.at[pl.ds(0, 5)])

    came(r_a.at[3, LATE], kall.at[pl.ds(0, LB)])

    zero_at = 0
    for j in range(NS):
        zero_at += jnp.where(so[0, j] == 0, j, 0)
    ones = jnp.ones((BLK, HD), F32)

    def put(slot, valid, key, value, first):
        rows = pl.ds(slot * BLK, BLK)
        kept = jnp.where(valid, 1.0, 0.0)
        key = key.reshape(BLK, HD).astype(F32)
        value = value.reshape(BLK, HD).astype(F32)
        if first is not None:
            key = key * kept + first * (1.0 - kept)
            value = value * kept
        ksel[rows, :] = key.astype(BF16)
        vsel[rows, pl.ds(0, HD)] = value.astype(BF16)
        vsel[rows, pl.ds(HD, HD)] = (ones * kept).astype(BF16)
        return key

    def select(i):
        block = ctx * LB + i
        key = put(0, True, kall[i], vall[i], None)
        first = jnp.broadcast_to(key[0:1, :], (BLK, HD))
        for j in range(NS - 1):
            off = so[0, j + jnp.where(zero_at <= j, 1, 0)]
            back = (off - i + LB - 1) // LB
            at = LB * back + (i - off + LB * back)
            put(1 + j, block - off >= 0, kall[at], vall[at], first)
        for j in range(NV):
            seen = vb[0, j]
            valid = seen < block
            for o in range(NS):
                valid = valid & (seen != block - so[0, o])
            put(NS + j, valid, vert[j, 0], vert[j, 1], first)

    def block_of(n):
        return LB - 1 - n // 2

    def attend(n):
        for g in range(GROUP):
            rows = pl.ds(block_of(n) * BLK + lax.rem(n, 2) * HALF, HALF)
            qs[pl.ds(g * HALF, HALF), :] = q[rows, pl.ds(g * HD, HD)]
        top = None
        for j in range(KEYS // 256):
            cols = pl.ds(j * 256, 256)
            part = lax.dot_general(
                qs[...], ksel[cols, :], (((1,), (1,)), ((), ())), preferred_element_type=F32
            )
            if j == 0:
                row = lax.rem(lax.broadcasted_iota(jnp.int32, part.shape, 0), HALF)
                row += lax.rem(n, 2) * HALF
                col_at = lax.broadcasted_iota(jnp.int32, part.shape, 1)
                part = jnp.where((col_at <= row) | (col_at >= BLK), part, -1e30)
            s[:, cols] = part
            two = jnp.maximum(part[:, :HD], part[:, HD:])
            top = two if top is None else jnp.maximum(top, two)
        top = jnp.max(top, axis=1, keepdims=True)
        for j in range(KEYS // 256):
            cols = pl.ds(j * 256, 256)
            p[:, cols] = jnp.exp2((s[:, cols] - top) * SCALE).astype(BF16)
        total = jnp.dot(p[...], vsel[...], preferred_element_type=F32)
        total = (total[:, :HD] / total[:, HD:]).astype(BF16)
        for g in range(GROUP):
            att[head, n, :, pl.ds(g * HD, HD)] = total[g * HALF : (g + 1) * HALF, :]

    part = HALF // 2

    def own(m, n):
        here = att.at[head, n]
        where = (right, left, other)[m]
        recv = r_p.at[n // 2] if m == 2 else r_d.at[0, n]
        return remote(here, here, s_d.at[0], recv, where)

    def chunk(m, n):
        return att.at[lax.rem(x + (X - 1, 1, 2)[m], X) * 2 + c, n]

    def share(m, n):
        here = chunk(m, n)
        return remote(here, here, s_d.at[0], r_p.at[n // 2], other)

    def relay_near(n, split=False):
        remote(att.at[0, pl.ds(0, 2)], att.at[0, pl.ds(0, 2)], s_d.at[0], r_d.at[0, n], right).wait_recv()
        for m in range(2):
            if split:
                here = chunk(m, n).at[pl.ds((0, part)[m], part)]
                remote(here, here, s_d.at[0], r_d.at[1, n], (right, left)[m]).start()
            else:

                @pl.when(lax.rem(n, 2) == m)
                def _():
                    here = chunk(m, n)
                    remote(here, here, s_d.at[0], r_d.at[1, n], (right, left)[m]).start()

        share(0, n).start()
        share(1, n).start()

    def relay_far(n):
        here = chunk(2, n)
        remote(here, here, s_d.at[0], r_d.at[1, n], right).wait_recv()
        share(2, n).start()

    def project(i):
        remote(att.at[0], att.at[0], s_d.at[0], r_p.at[i], other).wait_recv()
        total = jnp.zeros((BLK, 512), F32)
        for h in range(2 * X):
            rows = att[h, pl.ds(2 * i, 2)].reshape(BLK, 512)
            total += jnp.dot(rows, w[pl.ds(h * 512, 512), :], preferred_element_type=F32)
        out[pl.ds((LB - 1 - i) * BLK, BLK), :] = total.astype(BF16)

    def one_chunk(n):
        @pl.when(n == CHUNKS // 2)
        def _():
            came(r_a.at[3, EARLY], kall.at[pl.ds(0, LB)])
            for kv in range(2):
                (kall, vall)[kv][pl.ds(LB * 4, 2)] = rest[kv]

        @pl.when(lax.rem(n, 2) == 0)
        def _():
            select(block_of(n))

        attend(n)
        for m in range(3):
            own(m, n).start()

        @pl.when(n == 0)
        def _():
            relay(3, False)

        @pl.when(n >= 3)
        def _():
            relay_near(n - 3)

    each(0, CHUNKS, one_chunk)

    def sent_early():
        piece = BLK // Y * HD // 512
        message = 2 * BLK * HD // 512
        rows = (Y - 1) * 2 * LB * piece + (Z - 1) * 2 * 2 * piece + NV * 7 * 2 * piece + 16 * message
        for here, more in ((first_z, 10), (last_z, 6), (jnp.logical_not(first_z | last_z), 0)):

            @pl.when(here)
            def _():
                left_all(s_early.at[0], w.at[pl.ds(0, rows + more * message)])

    sent_early()
    each(0, 3, relay_far)
    relay_near(5)
    relay_far(3)
    relay_near(6)
    relay_near(CHUNKS - 1, split=True)
    project(0)
    relay_far(4)
    relay_far(5)
    project(1)
    relay_far(6)
    relay_far(7)
    project(2)
    project(3)
    left_all(s_d.at[0], w.at[pl.ds(0, 7 * 512)])


def body(sizes, queries, keys, values, vertical_blocks, slash_offsets, out_weight):
    Y, Z, X = sizes
    hbm = pl.BlockSpec(memory_space=pltpu.HBM)
    dma = pltpu.SemaphoreType.DMA
    piece = BLK // Y
    return pl.pallas_call(
        functools.partial(kernel, sizes),
        out_shape=jax.ShapeDtypeStruct((ROWS, 512), BF16),
        in_specs=[hbm] * 6,
        out_specs=pl.BlockSpec(memory_space=pltpu.VMEM),
        scratch_shapes=[
            pltpu.VMEM((ROWS, 512), BF16),
            pltpu.VMEM(out_weight.shape, BF16),
            pltpu.VMEM((5 * LB, Y, piece, HD), BF16),
            pltpu.VMEM((5 * LB, Y, piece, HD), BF16),
            pltpu.VMEM((2, 2, Y, piece, HD), BF16),
            pltpu.VMEM((4, 2, 2, 2, Y, piece, HD), BF16),
            pltpu.VMEM((2, Y, LB, piece, HD), BF16),
            pltpu.VMEM((NV, 2, piece, HD), BF16),
            pltpu.VMEM((NV, 2, piece, HD), BF16),
            pltpu.VMEM((NV, 2, Y, piece, HD), BF16),
            pltpu.VMEM((GROUP * HALF, HD), BF16),
            pltpu.VMEM((KEYS, HD), BF16),
            pltpu.VMEM((KEYS, 2 * HD), BF16),
            pltpu.VMEM((GROUP * HALF, KEYS), F32),
            pltpu.VMEM((GROUP * HALF, KEYS), BF16),
            pltpu.VMEM((2 * X, CHUNKS, HALF, 512), BF16),
            pltpu.SMEM((1, NV), jnp.int32),
            pltpu.SMEM((1, NS), jnp.int32),
            dma((6,)),
            dma((1,)),
            dma((4, 2)),
            dma((4, 2)),
            dma((1,)),
            dma((1,)),
            dma((Z // 2 + 1,)),
            dma((Z // 2 + 1,)),
            dma((1,)),
            dma((1,)),
            dma((2, CHUNKS)),
            dma((LB,)),
        ],
        compiler_params=pltpu.CompilerParams(
            collective_id=0, has_side_effects=True, vmem_limit_bytes=56_000_000
        ),
    )(
        *(
            pltpu.with_memory_space_constraint(value, pltpu.HBM)
            for value in (
                queries,
                keys.reshape(LB, Y, piece, HD),
                values.reshape(LB, Y, piece, HD),
                vertical_blocks,
                slash_offsets,
                out_weight,
            )
        )
    )


def solution(mesh):
    sizes = (8, 8, 4)
    torus = Mesh(mesh.devices.reshape(*sizes, 2), ("y", "z", "x", "core"))
    ctx, heads = ("y", "z"), ("x", "core")
    return jax.shard_map(
        functools.partial(body, sizes),
        mesh=torus,
        in_specs=(
            P(ctx, heads),
            P(ctx, heads),
            P(ctx, heads),
            P(heads, None),
            P(heads, None),
            P(None, heads),
        ),
        out_specs=P(ctx, heads),
        check_vma=False,
    )
```

```python
import functools
import math

import jax
import jax.numpy as jnp
from jax import lax
from jax.experimental import pallas as pl
from jax.experimental.pallas import tpu as pltpu
from jax.sharding import Mesh
from jax.sharding import PartitionSpec as P

HD = 128
BLK = 128
LB = 4
GROUP = 4
NV = 8
NS = 8
ROWS = LB * BLK
HALF = BLK // 2
CHUNKS = ROWS // HALF
KEYS = (NV + NS) * BLK
SCALE = math.log2(math.e) / math.sqrt(HD)
MESH = pl.DeviceIdType.MESH
BF16 = jnp.bfloat16
F32 = jnp.float32


def remote(src, dst, send, recv, where):
    return pltpu.make_async_remote_copy(
        src_ref=src, dst_ref=dst, send_sem=send, recv_sem=recv, device_id=where, device_id_type=MESH
    )


def each(lo, hi, do):
    def step(i, carry):
        do(i)
        return carry

    lax.fori_loop(lo, hi, step, 0)


def kernel(
    sizes,
    q_hbm,
    k_hbm,
    v_hbm,
    vb_hbm,
    so_hbm,
    w_hbm,
    out,
    q,
    w,
    kall,
    vall,
    rest,
    thru,
    st1,
    sel,
    st2,
    vert,
    qs,
    ksel,
    vsel,
    s,
    p,
    att,
    vb,
    so,
    s_loc,
    s_early,
    r_a,
    r_t,
    r_b1,
    r_b2,
    r_b3,
    r_b4,
    r_far,
    s_d,
    r_d,
    r_p,
):
    Y, Z, X = sizes
    y, z, x, c = (lax.axis_index(a) for a in ("y", "z", "x", "core"))
    ctx = y * Z + z
    head = x * 2 + c

    def at_y(i):
        return {"y": i}

    def at_z(i):
        return {"z": i}

    right, left = {"x": lax.rem(x + 1, X)}, {"x": lax.rem(x + X - 1, X)}
    other = {"core": 1 - c}

    tables = [
        pltpu.make_async_copy(vb_hbm, vb, s_loc.at[4]),
        pltpu.make_async_copy(so_hbm, so, s_loc.at[5]),
    ]
    for table in tables:
        table.start()
    barrier = pltpu.get_barrier_semaphore()

    def greet(where):
        pl.semaphore_signal(barrier, inc=1, device_id=where, device_id_type=MESH)

    each(1, Y, lambda d: greet(at_y(lax.rem(y + d, Y))))
    each(1, Z, lambda d: greet(at_z(lax.rem(z + d, Z))))
    for where in (right, left, other):
        greet(where)
    pl.semaphore_wait(barrier, Y - 1 + Z - 1 + 3)

    EARLY, LATE = 0, 1
    first_z, last_z = z == 0, z == Z - 1
    below = at_y(lax.rem(y + 1, Y))
    beyond = at_z(lax.rem(z + 1, Z))

    def by_last(d, half):
        return d >= 1 and half == LATE

    def window(d, kv, half):
        if d == 4 and half == EARLY:
            return rest.at[kv]
        return (kall, vall)[kv].at[pl.ds(LB * d + 2 * half, 2)]

    def source(d, kv, half):
        return (k_hbm, v_hbm)[kv].at[pl.ds(2 * half, 2)] if d == 0 else window(d, kv, half)

    def came(sem, bytes_of):
        remote(bytes_of, bytes_of, s_early.at[0], sem, beyond).wait_recv()

    def arrival(d, kv, half):
        return r_t.at[0 if d == 3 and half == LATE and kv == 1 else d, half]

    def send_hop(d, where, halves=(LATE, EARLY)):
        for last, here in ((False, jnp.logical_not(last_z)), (True, last_z)):

            @pl.when(here & where)
            def _():
                for half in halves:
                    if d > 0:
                        came(r_a.at[d - 1, half], kall.at[pl.ds(0, LB)])
                    for kv in range(2):
                        to, recv = window(d + 1, kv, half), r_a.at[d, half]
                        if last:
                            to, recv = thru.at[d, kv, half], arrival(d, kv, half)
                        target = below if last and by_last(d, half) else beyond
                        remote(source(d, kv, half), to, s_early.at[0], recv, target).start()

    def relay(d, last, halves=(LATE, EARLY)):
        @pl.when(last_z if last else first_z)
        def _():
            for half in halves:
                if by_last(d, half) == last:
                    apart = d == 3 and half == LATE
                    for kv in range(2):
                        if apart:
                            came(arrival(d, kv, half), kall.at[pl.ds(0, 2)])
                        elif kv == 0:
                            came(r_t.at[d, half], kall.at[pl.ds(0, LB)])
                        remote(
                            thru.at[d, kv, half],
                            window(d + 1, kv, half),
                            s_early.at[0],
                            r_a.at[d, half],
                            beyond if last else below,
                        ).start()

    def left_all(sem, bytes_of):
        remote(bytes_of, bytes_of, sem, r_a.at[0, 0], beyond).wait_send()

    def col(kv, to, frm):
        src = (k_hbm, v_hbm)[kv]
        return remote(src.at[:, to], st1.at[kv, frm], s_early.at[0], r_b1.at[0], at_y(to))

    def far_first(n, size):
        k = (n + 1) // 2
        return size // 2 + jnp.where(lax.rem(n, 2) == 0, k, -k)

    def send_col(n):
        to = lax.rem(y + far_first(n, Y), Y)
        col(0, to, y).start()
        col(1, to, y).start()

    each(0, Y - 1, send_col)
    send_hop(0, True)
    for src, to, sem in (
        (k_hbm.at[:, y], st1.at[0, y], 0),
        (v_hbm.at[:, y], st1.at[1, y], 0),
        (k_hbm, kall.at[pl.ds(0, LB)], 1),
        (v_hbm, vall.at[pl.ds(0, LB)], 1),
        (q_hbm, q, 2),
        (w_hbm, w, 3),
    ):
        pltpu.make_async_copy(src, to, s_loc.at[sem]).start()

    relay(0, False, (LATE,))
    send_hop(1, z > 0, (LATE,))
    pltpu.make_async_copy(st1.at[:, 0], st1.at[:, 0], s_loc.at[0]).wait()
    came(r_b1.at[0], st1.at[:, pl.ds(0, Y - 1)])

    for table in tables:
        table.wait()
    for j in range(NV):
        owner = vb[0, j] // LB
        for kv in range(2):
            sel[j, kv] = st1[kv, owner // Z, lax.rem(vb[0, j], LB)]

    def to_row(to, frm):
        return remote(sel.at[to], st2.at[frm], s_early.at[0], r_b2.at[0], at_z(to))

    each(0, Z - 1, lambda n: to_row(lax.rem(z + far_first(n, Z), Z), z).start())
    st2[z] = sel[z]

    relay(0, False, (EARLY,))
    send_hop(1, z > 0, (EARLY,))
    came(r_b2.at[0], st2.at[pl.ds(0, Z - 1)])

    vert[z, :, y] = st2[lax.rem(vb[0, z] // LB, Z)]

    def along(d):
        here = vert.at[z, :, y]
        to = at_z(lax.rem(z + d, Z))
        remote(here, here, s_early.at[0], r_b3.at[jnp.minimum(d, Z - d)], to).start()

    def spread(slot, to, frm, recv):
        here = vert.at[slot, :, frm]
        remote(here, here, s_early.at[0], recv, at_y(to)).start()

    def beside(d):
        if isinstance(d, int) and d in (0, Z // 2):
            return (lax.rem(z + d, Z),)
        return (lax.rem(z + d, Z), lax.rem(z + Z - d, Z))

    def spread_near(d):
        for slot in beside(d):
            for n in range(2):
                one, two = (lax.rem(y + (k, Y - k)[n], Y) for k in (1, 2))
                spread(slot, two, y, r_b4.at[d])
                spread(slot, one, y, r_far.at[0])

    def spread_far(d):
        came(r_b4.at[d], st2.at[pl.ds(0, 2 * len(beside(d)))])
        for slot in beside(d):
            for n in range(2):
                frm = lax.rem(y + (Y - 2, 2)[n], Y)
                one, two = (lax.rem(y + (k, Y - k)[n], Y) for k in (1, 2))

                @pl.when(lax.rem(slot, 2) == n)
                def _():
                    spread(slot, two, frm, r_far.at[0])

                spread(slot, one, frm, r_far.at[0])

    def pass_on(d):
        came(r_b3.at[d], st2.at[pl.ds(0, len(beside(d)))])
        spread_near(d)

    each(0, Z - 1, lambda n: along(far_first(n, Z)))
    spread_near(0)
    send_hop(1, first_z, (LATE,))
    relay(1, True)
    relay(1, False)
    send_hop(2, z >= 2)

    pass_on(1)
    send_hop(1, first_z, (EARLY,))
    pass_on(2)
    spread_far(0)
    pass_on(3)
    pass_on(4)
    send_hop(2, z < 2, (LATE,))
    send_hop(3, z >= 3, (LATE,))
    relay(2, True)
    for d in range(1, 5):
        spread_far(d)
    relay(2, False)
    send_hop(2, z < 2, (EARLY,))
    send_hop(3, z < 3, (LATE,))
    relay(3, True)
    send_hop(3, True, (EARLY,))
    pltpu.make_async_copy(thru.at[0], thru.at[0], s_loc.at[1]).wait()
    pltpu.make_async_copy(q_hbm, q, s_loc.at[2]).wait()
    pltpu.make_async_copy(w_hbm, w, s_loc.at[3]).wait()

    came(r_far.at[0], vert.at[pl.ds(0, 5)])

    came(r_a.at[3, LATE], kall.at[pl.ds(0, LB)])

    zero_at = 0
    for j in range(NS):
        zero_at += jnp.where(so[0, j] == 0, j, 0)
    ones = jnp.ones((BLK, HD), F32)

    def put(slot, valid, key, value, first):
        rows = pl.ds(slot * BLK, BLK)
        kept = jnp.where(valid, 1.0, 0.0)
        key = key.reshape(BLK, HD).astype(F32)
        value = value.reshape(BLK, HD).astype(F32)
        if first is not None:
            key = key * kept + first * (1.0 - kept)
            value = value * kept
        ksel[rows, :] = key.astype(BF16)
        vsel[rows, pl.ds(0, HD)] = value.astype(BF16)
        vsel[rows, pl.ds(HD, HD)] = (ones * kept).astype(BF16)
        return key

    def select(i):
        block = ctx * LB + i
        key = put(0, True, kall[i], vall[i], None)
        first = jnp.broadcast_to(key[0:1, :], (BLK, HD))
        for j in range(NS - 1):
            off = so[0, j + jnp.where(zero_at <= j, 1, 0)]
            back = (off - i + LB - 1) // LB
            at = LB * back + (i - off + LB * back)
            put(1 + j, block - off >= 0, kall[at], vall[at], first)
        for j in range(NV):
            seen = vb[0, j]
            valid = seen < block
            for o in range(NS):
                valid = valid & (seen != block - so[0, o])
            put(NS + j, valid, vert[j, 0], vert[j, 1], first)

    def block_of(n):
        return LB - 1 - n // 2

    def attend(n):
        for g in range(GROUP):
            rows = pl.ds(block_of(n) * BLK + lax.rem(n, 2) * HALF, HALF)
            qs[pl.ds(g * HALF, HALF), :] = q[rows, pl.ds(g * HD, HD)]
        top = None
        for j in range(KEYS // 256):
            cols = pl.ds(j * 256, 256)
            part = lax.dot_general(
                qs[...], ksel[cols, :], (((1,), (1,)), ((), ())), preferred_element_type=F32
            )
            if j == 0:
                row = lax.rem(lax.broadcasted_iota(jnp.int32, part.shape, 0), HALF)
                row += lax.rem(n, 2) * HALF
                col_at = lax.broadcasted_iota(jnp.int32, part.shape, 1)
                part = jnp.where((col_at <= row) | (col_at >= BLK), part, -1e30)
            s[:, cols] = part
            two = jnp.maximum(part[:, :HD], part[:, HD:])
            top = two if top is None else jnp.maximum(top, two)
        top = jnp.max(top, axis=1, keepdims=True)
        for j in range(KEYS // 256):
            cols = pl.ds(j * 256, 256)
            p[:, cols] = jnp.exp2((s[:, cols] - top) * SCALE).astype(BF16)
        total = jnp.dot(p[...], vsel[...], preferred_element_type=F32)
        total = (total[:, :HD] / total[:, HD:]).astype(BF16)
        for g in range(GROUP):
            att[head, n, :, pl.ds(g * HD, HD)] = total[g * HALF : (g + 1) * HALF, :]

    part = HALF // 2

    def own(m, n):
        here = att.at[head, n]
        where = (right, left, other)[m]
        recv = r_p.at[n // 2] if m == 2 else r_d.at[0, n]
        return remote(here, here, s_d.at[0], recv, where)

    def chunk(m, n):
        return att.at[lax.rem(x + (X - 1, 1, 2)[m], X) * 2 + c, n]

    def share(m, n):
        here = chunk(m, n)
        late = isinstance(n, int) and n >= CHUNKS - 2 and m == 2
        return remote(here, here, s_d.at[0], r_p.at[LB if late else n // 2], other)

    def relay_near(n, split=False):
        remote(att.at[0, pl.ds(0, 2)], att.at[0, pl.ds(0, 2)], s_d.at[0], r_d.at[0, n], right).wait_recv()
        for m in range(2):
            if split:
                here = chunk(m, n).at[pl.ds((0, part)[m], part)]
                remote(here, here, s_d.at[0], r_d.at[1, n], (right, left)[m]).start()
            else:

                @pl.when(lax.rem(n, 2) == m)
                def _():
                    here = chunk(m, n)
                    remote(here, here, s_d.at[0], r_d.at[1, n], (right, left)[m]).start()

        share(0, n).start()
        share(1, n).start()

    def relay_far(n):
        here = chunk(2, n)
        remote(here, here, s_d.at[0], r_d.at[1, n], right).wait_recv()
        share(2, n).start()

    def project(i):
        last = i == LB - 1
        near = att.at[0, pl.ds(0, 6)] if last else att.at[0]
        remote(near, near, s_d.at[0], r_p.at[i], other).wait_recv()
        total = jnp.zeros((BLK, 512), F32)
        for h in range(2 * X):
            if last and h == 6:
                across = att.at[0, pl.ds(0, 2)]
                remote(across, across, s_d.at[0], r_p.at[LB], other).wait_recv()
            at = lax.rem(x + (0, 1, X - 1, 2)[h // 2], X) * 2 + h % 2
            rows = att[at, pl.ds(2 * i, 2)].reshape(BLK, 512)
            part_of = w[pl.ds(pl.multiple_of(at * 512, 512), 512), :]
            total += jnp.dot(rows, part_of, preferred_element_type=F32)
        out[pl.ds((LB - 1 - i) * BLK, BLK), :] = total.astype(BF16)

    def one_chunk(n):
        @pl.when(n == CHUNKS // 2)
        def _():
            came(r_a.at[3, EARLY], kall.at[pl.ds(0, LB)])
            for kv in range(2):
                (kall, vall)[kv][pl.ds(LB * 4, 2)] = rest[kv]

        @pl.when(lax.rem(n, 2) == 0)
        def _():
            select(block_of(n))

        attend(n)
        for m in range(3):
            own(m, n).start()

        @pl.when(n == 0)
        def _():
            relay(3, False)

        @pl.when(n >= 3)
        def _():
            relay_near(n - 3)

    each(0, CHUNKS, one_chunk)

    def sent_early():
        piece = BLK // Y * HD // 512
        message = 2 * BLK * HD // 512
        rows = (Y - 1) * 2 * LB * piece + (Z - 1) * 2 * 2 * piece + NV * 7 * 2 * piece + 16 * message
        for here, more in ((first_z, 10), (last_z, 6), (jnp.logical_not(first_z | last_z), 0)):

            @pl.when(here)
            def _():
                left_all(s_early.at[0], w.at[pl.ds(0, rows + more * message)])

    sent_early()
    each(0, 3, relay_far)
    relay_near(5)
    relay_far(3)
    relay_near(6)
    relay_near(CHUNKS - 1, split=True)
    project(0)
    relay_far(4)
    relay_far(5)
    project(1)
    relay_far(6)
    relay_far(7)
    project(2)
    project(3)
    left_all(s_d.at[0], w.at[pl.ds(0, 7 * 512)])


def body(sizes, queries, keys, values, vertical_blocks, slash_offsets, out_weight):
    Y, Z, X = sizes
    hbm = pl.BlockSpec(memory_space=pltpu.HBM)
    dma = pltpu.SemaphoreType.DMA
    piece = BLK // Y
    return pl.pallas_call(
        functools.partial(kernel, sizes),
        out_shape=jax.ShapeDtypeStruct((ROWS, 512), BF16),
        in_specs=[hbm] * 6,
        out_specs=pl.BlockSpec(memory_space=pltpu.VMEM),
        scratch_shapes=[
            pltpu.VMEM((ROWS, 512), BF16),
            pltpu.VMEM(out_weight.shape, BF16),
            pltpu.VMEM((5 * LB, Y, piece, HD), BF16),
            pltpu.VMEM((5 * LB, Y, piece, HD), BF16),
            pltpu.VMEM((2, 2, Y, piece, HD), BF16),
            pltpu.VMEM((4, 2, 2, 2, Y, piece, HD), BF16),
            pltpu.VMEM((2, Y, LB, piece, HD), BF16),
            pltpu.VMEM((NV, 2, piece, HD), BF16),
            pltpu.VMEM((NV, 2, piece, HD), BF16),
            pltpu.VMEM((NV, 2, Y, piece, HD), BF16),
            pltpu.VMEM((GROUP * HALF, HD), BF16),
            pltpu.VMEM((KEYS, HD), BF16),
            pltpu.VMEM((KEYS, 2 * HD), BF16),
            pltpu.VMEM((GROUP * HALF, KEYS), F32),
            pltpu.VMEM((GROUP * HALF, KEYS), BF16),
            pltpu.VMEM((2 * X, CHUNKS, HALF, 512), BF16),
            pltpu.SMEM((1, NV), jnp.int32),
            pltpu.SMEM((1, NS), jnp.int32),
            dma((6,)),
            dma((1,)),
            dma((4, 2)),
            dma((4, 2)),
            dma((1,)),
            dma((1,)),
            dma((Z // 2 + 1,)),
            dma((Z // 2 + 1,)),
            dma((1,)),
            dma((1,)),
            dma((2, CHUNKS)),
            dma((LB + 1,)),
        ],
        compiler_params=pltpu.CompilerParams(
            collective_id=0, has_side_effects=True, vmem_limit_bytes=56_000_000
        ),
    )(
        *(
            pltpu.with_memory_space_constraint(value, pltpu.HBM)
            for value in (
                queries,
                keys.reshape(LB, Y, piece, HD),
                values.reshape(LB, Y, piece, HD),
                vertical_blocks,
                slash_offsets,
                out_weight,
            )
        )
    )


def solution(mesh):
    sizes = (8, 8, 4)
    torus = Mesh(mesh.devices.reshape(*sizes, 2), ("y", "z", "x", "core"))
    ctx, heads = ("y", "z"), ("x", "core")
    return jax.shard_map(
        functools.partial(body, sizes),
        mesh=torus,
        in_specs=(
            P(ctx, heads),
            P(ctx, heads),
            P(ctx, heads),
            P(heads, None),
            P(heads, None),
            P(None, heads),
        ),
        out_specs=P(ctx, heads),
        check_vma=False,
    )
```

```python
import functools
import math

import jax
import jax.numpy as jnp
from jax import lax
from jax.experimental import pallas as pl
from jax.experimental.pallas import tpu as pltpu
from jax.sharding import Mesh
from jax.sharding import PartitionSpec as P

HD = 128
BLK = 128
LB = 4
GROUP = 4
NV = 8
NS = 8
ROWS = LB * BLK
HALF = BLK // 2
CHUNKS = ROWS // HALF
KEYS = (NV + NS) * BLK
SCALE = math.log2(math.e) / math.sqrt(HD)
MESH = pl.DeviceIdType.MESH
BF16 = jnp.bfloat16
F32 = jnp.float32


def remote(src, dst, send, recv, where):
    return pltpu.make_async_remote_copy(
        src_ref=src, dst_ref=dst, send_sem=send, recv_sem=recv, device_id=where, device_id_type=MESH
    )


def each(lo, hi, do):
    def step(i, carry):
        do(i)
        return carry

    lax.fori_loop(lo, hi, step, 0)


def kernel(
    sizes,
    q_hbm,
    k_hbm,
    v_hbm,
    vb_hbm,
    so_hbm,
    w_hbm,
    out,
    q,
    w,
    kall,
    vall,
    rest,
    thru,
    st1,
    sel,
    st2,
    vert,
    qs,
    ksel,
    vsel,
    s,
    p,
    att,
    vb,
    so,
    s_loc,
    s_early,
    r_a,
    r_t,
    r_b1,
    r_b2,
    r_b3,
    r_b4,
    r_far,
    s_d,
    r_d,
    r_p,
):
    Y, Z, X = sizes
    y, z, x, c = (lax.axis_index(a) for a in ("y", "z", "x", "core"))
    ctx = y * Z + z
    head = x * 2 + c

    def at_y(i):
        return {"y": i}

    def at_z(i):
        return {"z": i}

    right, left = {"x": lax.rem(x + 1, X)}, {"x": lax.rem(x + X - 1, X)}
    other = {"core": 1 - c}

    tables = [
        pltpu.make_async_copy(vb_hbm, vb, s_loc.at[4]),
        pltpu.make_async_copy(so_hbm, so, s_loc.at[5]),
    ]
    for table in tables:
        table.start()
    barrier = pltpu.get_barrier_semaphore()

    def greet(where):
        pl.semaphore_signal(barrier, inc=1, device_id=where, device_id_type=MESH)

    each(1, Y, lambda d: greet(at_y(lax.rem(y + d, Y))))
    each(1, Z, lambda d: greet(at_z(lax.rem(z + d, Z))))
    for where in (right, left, other):
        greet(where)
    pl.semaphore_wait(barrier, Y - 1 + Z - 1 + 3)

    EARLY, LATE = 0, 1
    first_z, last_z = z == 0, z == Z - 1
    below = at_y(lax.rem(y + 1, Y))
    beyond = at_z(lax.rem(z + 1, Z))

    def by_last(d, half):
        return d >= 1 and half == LATE

    def window(d, kv, half):
        if d == 4 and half == EARLY:
            return rest.at[kv]
        return (kall, vall)[kv].at[pl.ds(LB * d + 2 * half, 2)]

    def source(d, kv, half):
        return (k_hbm, v_hbm)[kv].at[pl.ds(2 * half, 2)] if d == 0 else window(d, kv, half)

    def came(sem, bytes_of):
        remote(bytes_of, bytes_of, s_early.at[0], sem, beyond).wait_recv()

    def arrival(d, kv, half):
        return r_t.at[0 if d == 3 and half == LATE and kv == 1 else d, half]

    def send_hop(d, where, halves=(LATE, EARLY)):
        for last, here in ((False, jnp.logical_not(last_z)), (True, last_z)):

            @pl.when(here & where)
            def _():
                for half in halves:
                    if d > 0:
                        came(r_a.at[d - 1, half], kall.at[pl.ds(0, LB)])
                    for kv in range(2):
                        to, recv = window(d + 1, kv, half), r_a.at[d, half]
                        if last:
                            to, recv = thru.at[d, kv, half], arrival(d, kv, half)
                        target = below if last and by_last(d, half) else beyond
                        remote(source(d, kv, half), to, s_early.at[0], recv, target).start()

    def relay(d, last, halves=(LATE, EARLY)):
        @pl.when(last_z if last else first_z)
        def _():
            for half in halves:
                if by_last(d, half) == last:
                    apart = d == 3 and half == LATE
                    for kv in range(2):
                        if apart:
                            came(arrival(d, kv, half), kall.at[pl.ds(0, 2)])
                        elif kv == 0:
                            came(r_t.at[d, half], kall.at[pl.ds(0, LB)])
                        remote(
                            thru.at[d, kv, half],
                            window(d + 1, kv, half),
                            s_early.at[0],
                            r_a.at[d, half],
                            beyond if last else below,
                        ).start()

    def left_all(sem, bytes_of):
        remote(bytes_of, bytes_of, sem, r_a.at[0, 0], beyond).wait_send()

    def col(kv, to, frm):
        src = (k_hbm, v_hbm)[kv]
        return remote(src.at[:, to], st1.at[kv, frm], s_early.at[0], r_b1.at[0], at_y(to))

    def far_first(n, size):
        k = (n + 1) // 2
        return size // 2 + jnp.where(lax.rem(n, 2) == 0, k, -k)

    def send_col(n):
        to = lax.rem(y + far_first(n, Y), Y)
        col(0, to, y).start()
        col(1, to, y).start()

    each(0, Y - 1, send_col)
    send_hop(0, True)
    for src, to, sem in (
        (k_hbm.at[:, y], st1.at[0, y], 0),
        (v_hbm.at[:, y], st1.at[1, y], 0),
        (k_hbm, kall.at[pl.ds(0, LB)], 1),
        (v_hbm, vall.at[pl.ds(0, LB)], 1),
        (q_hbm, q, 2),
        (w_hbm, w, 3),
    ):
        pltpu.make_async_copy(src, to, s_loc.at[sem]).start()

    relay(0, False, (LATE,))
    send_hop(1, z > 0, (LATE,))
    pltpu.make_async_copy(st1.at[:, 0], st1.at[:, 0], s_loc.at[0]).wait()
    came(r_b1.at[0], st1.at[:, pl.ds(0, Y - 1)])

    for table in tables:
        table.wait()
    for j in range(NV):
        owner = vb[0, j] // LB
        for kv in range(2):
            sel[j, kv] = st1[kv, owner // Z, lax.rem(vb[0, j], LB)]

    def to_row(to, frm):
        return remote(sel.at[to], st2.at[frm], s_early.at[0], r_b2.at[0], at_z(to))

    each(0, Z - 1, lambda n: to_row(lax.rem(z + far_first(n, Z), Z), z).start())
    st2[z] = sel[z]

    relay(0, False, (EARLY,))
    send_hop(1, z > 0, (EARLY,))
    came(r_b2.at[0], st2.at[pl.ds(0, Z - 1)])

    vert[z, :, y] = st2[lax.rem(vb[0, z] // LB, Z)]

    def along(d):
        here = vert.at[z, :, y]
        to = at_z(lax.rem(z + d, Z))
        remote(here, here, s_early.at[0], r_b3.at[jnp.minimum(d, Z - d)], to).start()

    def spread(slot, to, frm, recv):
        here = vert.at[slot, :, frm]
        remote(here, here, s_early.at[0], recv, at_y(to)).start()

    def beside(d):
        if isinstance(d, int) and d in (0, Z // 2):
            return (lax.rem(z + d, Z),)
        return (lax.rem(z + d, Z), lax.rem(z + Z - d, Z))

    def spread_near(d):
        for slot in beside(d):
            for n in range(2):
                one, two = (lax.rem(y + (k, Y - k)[n], Y) for k in (1, 2))
                spread(slot, two, y, r_b4.at[d])
                spread(slot, one, y, r_far.at[0])

    def spread_far(d):
        came(r_b4.at[d], st2.at[pl.ds(0, 2 * len(beside(d)))])
        for slot in beside(d):
            for n in range(2):
                frm = lax.rem(y + (Y - 2, 2)[n], Y)
                one, two = (lax.rem(y + (k, Y - k)[n], Y) for k in (1, 2))

                @pl.when(lax.rem(slot, 2) == n)
                def _():
                    spread(slot, two, frm, r_far.at[0])

                spread(slot, one, frm, r_far.at[0])

    def pass_on(d):
        came(r_b3.at[d], st2.at[pl.ds(0, len(beside(d)))])
        spread_near(d)

    each(0, Z - 1, lambda n: along(far_first(n, Z)))
    spread_near(0)
    send_hop(1, first_z, (LATE,))
    relay(1, True)
    relay(1, False)
    send_hop(2, z >= 2)

    pass_on(1)
    send_hop(1, first_z, (EARLY,))
    pass_on(2)
    spread_far(0)
    pass_on(3)
    pass_on(4)
    send_hop(2, z < 2, (LATE,))
    send_hop(3, z >= 3, (LATE,))
    relay(2, True)
    for d in range(1, 5):
        spread_far(d)
    relay(2, False)
    send_hop(2, z < 2, (EARLY,))
    send_hop(3, z < 3, (LATE,))
    relay(3, True)
    send_hop(3, True, (EARLY,))
    pltpu.make_async_copy(thru.at[0], thru.at[0], s_loc.at[1]).wait()
    pltpu.make_async_copy(q_hbm, q, s_loc.at[2]).wait()
    pltpu.make_async_copy(w_hbm, w, s_loc.at[3]).wait()

    came(r_far.at[0], vert.at[pl.ds(0, 5)])

    came(r_a.at[3, LATE], kall.at[pl.ds(0, LB)])

    zero_at = 0
    for j in range(NS):
        zero_at += jnp.where(so[0, j] == 0, j, 0)
    ones = jnp.ones((BLK, HD), F32)

    def put(slot, valid, key, value, first):
        rows = pl.ds(slot * BLK, BLK)
        kept = jnp.where(valid, 1.0, 0.0)
        key = key.reshape(BLK, HD).astype(F32)
        value = value.reshape(BLK, HD).astype(F32)
        if first is not None:
            key = key * kept + first * (1.0 - kept)
            value = value * kept
        ksel[rows, :] = key.astype(BF16)
        vsel[rows, pl.ds(0, HD)] = value.astype(BF16)
        vsel[rows, pl.ds(HD, HD)] = (ones * kept).astype(BF16)
        return key

    def select(i):
        block = ctx * LB + i
        key = put(0, True, kall[i], vall[i], None)
        first = jnp.broadcast_to(key[0:1, :], (BLK, HD))
        for j in range(NS - 1):
            off = so[0, j + jnp.where(zero_at <= j, 1, 0)]
            back = (off - i + LB - 1) // LB
            at = LB * back + (i - off + LB * back)
            put(1 + j, block - off >= 0, kall[at], vall[at], first)
        for j in range(NV):
            seen = vb[0, j]
            valid = seen < block
            for o in range(NS):
                valid = valid & (seen != block - so[0, o])
            put(NS + j, valid, vert[j, 0], vert[j, 1], first)

    def block_of(n):
        return LB - 1 - n // 2

    def attend(n):
        for g in range(GROUP):
            rows = pl.ds(block_of(n) * BLK + lax.rem(n, 2) * HALF, HALF)
            qs[pl.ds(g * HALF, HALF), :] = q[rows, pl.ds(g * HD, HD)]
        top = None
        for j in range(KEYS // 256):
            cols = pl.ds(j * 256, 256)
            part = lax.dot_general(
                qs[...], ksel[cols, :], (((1,), (1,)), ((), ())), preferred_element_type=F32
            )
            if j == 0:
                row = lax.rem(lax.broadcasted_iota(jnp.int32, part.shape, 0), HALF)
                row += lax.rem(n, 2) * HALF
                col_at = lax.broadcasted_iota(jnp.int32, part.shape, 1)
                part = jnp.where((col_at <= row) | (col_at >= BLK), part, -1e30)
            s[:, cols] = part
            two = jnp.maximum(part[:, :HD], part[:, HD:])
            top = two if top is None else jnp.maximum(top, two)
        top = jnp.max(top, axis=1, keepdims=True)
        for j in range(KEYS // 256):
            cols = pl.ds(j * 256, 256)
            p[:, cols] = jnp.exp2((s[:, cols] - top) * SCALE).astype(BF16)
        total = jnp.dot(p[...], vsel[...], preferred_element_type=F32)
        total = (total[:, :HD] / total[:, HD:]).astype(BF16)
        for g in range(GROUP):
            att[head, n, :, pl.ds(g * HD, HD)] = total[g * HALF : (g + 1) * HALF, :]

    part = HALF // 2

    def own(m, n):
        here = att.at[head, n]
        where = (right, left, other)[m]
        recv = r_p.at[n // 2] if m == 2 else r_d.at[0, n]
        return remote(here, here, s_d.at[0], recv, where)

    def chunk(m, n):
        return att.at[lax.rem(x + (X - 1, 1, 2)[m], X) * 2 + c, n]

    def share(m, n):
        here = chunk(m, n)
        late = isinstance(n, int) and n >= CHUNKS - 2 and m == 2
        return remote(here, here, s_d.at[0], r_p.at[LB if late else n // 2], other)

    def relay_near(n, split=False):
        remote(att.at[0, pl.ds(0, 2)], att.at[0, pl.ds(0, 2)], s_d.at[0], r_d.at[0, n], right).wait_recv()
        for m in range(2):
            if split:
                here = chunk(m, n).at[pl.ds((0, part)[m], part)]
                remote(here, here, s_d.at[0], r_d.at[1, n], (right, left)[m]).start()
            else:

                @pl.when(lax.rem(n, 2) == m)
                def _():
                    here = chunk(m, n)
                    remote(here, here, s_d.at[0], r_d.at[1, n], (right, left)[m]).start()

        share(0, n).start()
        share(1, n).start()

    def relay_far(n):
        here = chunk(2, n)
        remote(here, here, s_d.at[0], r_d.at[1, n], right).wait_recv()
        share(2, n).start()

    def project(i):
        last = i == LB - 1
        near = att.at[0, pl.ds(0, 6)] if last else att.at[0]
        remote(near, near, s_d.at[0], r_p.at[i], other).wait_recv()
        total = jnp.zeros((BLK, 512), F32)
        for h in range(2 * X):
            if last and h == 6:
                across = att.at[0, pl.ds(0, 2)]
                remote(across, across, s_d.at[0], r_p.at[LB], other).wait_recv()
            at = lax.rem(x + (0, 1, X - 1, 2)[h // 2], X) * 2 + h % 2
            rows = att[at, pl.ds(2 * i, 2)].reshape(BLK, 512)
            part_of = w[pl.ds(pl.multiple_of(at * 512, 512), 512), :]
            total += jnp.dot(rows, part_of, preferred_element_type=F32)
        out[pl.ds((LB - 1 - i) * BLK, BLK), :] = total.astype(BF16)

    def one_chunk(n):
        @pl.when(n == CHUNKS // 2)
        def _():
            came(r_a.at[3, EARLY], kall.at[pl.ds(0, LB)])
            for kv in range(2):
                (kall, vall)[kv][pl.ds(LB * 4, 2)] = rest[kv]

        @pl.when(lax.rem(n, 2) == 0)
        def _():
            select(block_of(n))

        attend(n)
        for m in range(3):
            own(m, n).start()

        @pl.when(n == 0)
        def _():
            relay(3, False)

        @pl.when(n >= 3)
        def _():
            relay_near(n - 3)

    each(0, CHUNKS, one_chunk)

    def sent_early():
        piece = BLK // Y * HD // 512
        message = 2 * BLK * HD // 512
        rows = (Y - 1) * 2 * LB * piece + (Z - 1) * 2 * 2 * piece + NV * 7 * 2 * piece + 16 * message
        for here, more in ((first_z, 10), (last_z, 6), (jnp.logical_not(first_z | last_z), 0)):

            @pl.when(here)
            def _():
                left_all(s_early.at[0], w.at[pl.ds(0, rows + more * message)])

    sent_early()
    relay_near(5)
    each(0, 3, relay_far)
    relay_far(3)
    relay_near(6, split=True)
    relay_near(CHUNKS - 1, split=True)
    project(0)
    relay_far(4)
    relay_far(5)
    project(1)
    relay_far(6)
    relay_far(7)
    project(2)
    project(3)
    left_all(s_d.at[0], w.at[pl.ds(0, 7 * 512)])


def body(sizes, queries, keys, values, vertical_blocks, slash_offsets, out_weight):
    Y, Z, X = sizes
    hbm = pl.BlockSpec(memory_space=pltpu.HBM)
    dma = pltpu.SemaphoreType.DMA
    piece = BLK // Y
    return pl.pallas_call(
        functools.partial(kernel, sizes),
        out_shape=jax.ShapeDtypeStruct((ROWS, 512), BF16),
        in_specs=[hbm] * 6,
        out_specs=pl.BlockSpec(memory_space=pltpu.VMEM),
        scratch_shapes=[
            pltpu.VMEM((ROWS, 512), BF16),
            pltpu.VMEM(out_weight.shape, BF16),
            pltpu.VMEM((5 * LB, Y, piece, HD), BF16),
            pltpu.VMEM((5 * LB, Y, piece, HD), BF16),
            pltpu.VMEM((2, 2, Y, piece, HD), BF16),
            pltpu.VMEM((4, 2, 2, 2, Y, piece, HD), BF16),
            pltpu.VMEM((2, Y, LB, piece, HD), BF16),
            pltpu.VMEM((NV, 2, piece, HD), BF16),
            pltpu.VMEM((NV, 2, piece, HD), BF16),
            pltpu.VMEM((NV, 2, Y, piece, HD), BF16),
            pltpu.VMEM((GROUP * HALF, HD), BF16),
            pltpu.VMEM((KEYS, HD), BF16),
            pltpu.VMEM((KEYS, 2 * HD), BF16),
            pltpu.VMEM((GROUP * HALF, KEYS), F32),
            pltpu.VMEM((GROUP * HALF, KEYS), BF16),
            pltpu.VMEM((2 * X, CHUNKS, HALF, 512), BF16),
            pltpu.SMEM((1, NV), jnp.int32),
            pltpu.SMEM((1, NS), jnp.int32),
            dma((6,)),
            dma((1,)),
            dma((4, 2)),
            dma((4, 2)),
            dma((1,)),
            dma((1,)),
            dma((Z // 2 + 1,)),
            dma((Z // 2 + 1,)),
            dma((1,)),
            dma((1,)),
            dma((2, CHUNKS)),
            dma((LB + 1,)),
        ],
        compiler_params=pltpu.CompilerParams(
            collective_id=0, has_side_effects=True, vmem_limit_bytes=56_000_000
        ),
    )(
        *(
            pltpu.with_memory_space_constraint(value, pltpu.HBM)
            for value in (
                queries,
                keys.reshape(LB, Y, piece, HD),
                values.reshape(LB, Y, piece, HD),
                vertical_blocks,
                slash_offsets,
                out_weight,
            )
        )
    )


def solution(mesh):
    sizes = (8, 8, 4)
    torus = Mesh(mesh.devices.reshape(*sizes, 2), ("y", "z", "x", "core"))
    ctx, heads = ("y", "z"), ("x", "core")
    return jax.shard_map(
        functools.partial(body, sizes),
        mesh=torus,
        in_specs=(
            P(ctx, heads),
            P(ctx, heads),
            P(ctx, heads),
            P(heads, None),
            P(heads, None),
            P(None, heads),
        ),
        out_specs=P(ctx, heads),
        check_vma=False,
    )
```
